32 devices in a mesh: gx: 4 (over z), gy: 8 (over y, x, core).
Axes of the slice: x: 2, y: 2, z: 4, core: 2. Of those that a mesh axis runs over, the one named last changes fastest.
Arguments:
- particles: bfloat16 [2048, 4096], P(('gx', 'gy')), may hold values from -6 to 6
- references: bfloat16 [4, 12, 4096], P('gx'), may hold values from -1 to 1
- slot_class: int32 [4], replicated, may hold values from 0 to 3, each once
- log_prior: float32 [4], replicated, may hold values from -2 to 2
- shift_offsets: int32 [8, 2], replicated, may hold values from -8 to 8
- group_ids: int32 [2048], P(('gx', 'gy')), may hold values from 0 to 127
- ctf_table: float32 [128, 2048], replicated, may hold values from -1 to 1
- noise_power: float32 [2048], replicated, may hold values from 0.5 to 2
Outputs:
- class_sums: float32 [4, 12, 4096], P('gx')
- ctf_power: float32 [4, 2048], P('gx')
- log_evidence: float32 [], replicated
The draws below stay inside these ranges and needn't reach their ends.
Inputs may be any that keep to these rules, and one draw needn't show every extreme that they name: `slot_class`: each class id stands at exactly one slot.
All inputs are finite; a program needn't handle non-finite values.
Results may differ from the reference program's by a relative error of at most 0.006.
Values may be sent and summed in bfloat16 or wider, within the bound.
No kernel may reach another device: no remote copies, remote signals or barrier semaphores. Data moves between devices by JAX's collectives and lax.ppermute only.
A program may use at most 64 MiB of HBM per device.

```python
import math
import jax
import jax.numpy as jnp
from jax import lax

L = 64
R = 12
NS = 8
G = 128
PART_DEV = 64
HALF = 2048
FR = 4096
CLASSES = 4
PARTICLES = 2048
N_GX = 4
N_GY = 8


def plant(values, own_key, smallest, largest):
    longest = values.shape.index(max(values.shape))
    spots = []
    for shift in (0, 1):
        where = [jax.random.randint(jax.random.fold_in(own_key, axis), (), 0, length) for axis, length in enumerate(values.shape)]
        where[longest] = (where[longest] + shift) % values.shape[longest]
        spots.append(tuple(where))
    return values.at[spots[0]].set(smallest).at[spots[1]].set(largest)


def steps_of(key, shape, cuts, smallest, high):
    factor_of = 1.0
    for position, shards_of in cuts:
        draws = jax.random.uniform(jax.random.fold_in(jax.random.fold_in(key, 6), position), (shards_of,), jnp.float32, smallest / len(cuts), high / len(cuts))
        factor_of = factor_of * jnp.repeat(jnp.exp(draws), shape[position] // shards_of).reshape((-1,) + (1,) * (len(shape) - 1 - position))
    return factor_of


def gaussian(rng, extent, deviation, most, shards=(), held_as=jnp.bfloat16):
    array = deviation * jax.random.normal(rng, extent, jnp.float32)
    if shards:
        array = array * steps_of(rng, extent, shards, -0.22, 0.18)
    return jnp.clip(array, -most, most).astype(held_as)


def setup_inputs(seed: int = 0) -> dict:
    arg_keys = jax.random.split(jax.random.key(seed), 9)
    return {
        "particles": gaussian(arg_keys[0], (PARTICLES, L * L), 1.0, 6.0, ((0, 32),)),
        "references": gaussian(arg_keys[1], (CLASSES, R, FR), 0.07, 1.0, ((0, 4),)),
        "slot_class": jax.random.permutation(arg_keys[2], CLASSES).astype(jnp.int32),
        "log_prior": jnp.clip(jax.random.uniform(arg_keys[3], (CLASSES,), jnp.float32, -2.0, 2.0), -2.0, 2.0),
        "shift_offsets": plant(jax.random.randint(arg_keys[4], (NS, 2), -8, 9), jax.random.fold_in(arg_keys[4], 1), -8, 8).astype(jnp.int32),
        "group_ids": plant(jax.random.randint(arg_keys[5], (PARTICLES,), 0, G), jax.random.fold_in(arg_keys[5], 1), 0, G - 1).astype(jnp.int32),
        "ctf_table": jnp.clip(jax.random.uniform(arg_keys[6], (G, HALF), jnp.float32, -1.0, 1.0), -1.0, 1.0),
        "noise_power": jnp.clip(jnp.exp(jax.random.uniform(arg_keys[7], (HALF,), jnp.float32, math.log(0.5), math.log(2.0))), 0.5, 2.0),
    }


def phase_tables(shift_offsets, edge_len):
    half_size = edge_len * edge_len // 2
    freq_index = jnp.arange(half_size, dtype=jnp.int32)
    row_freq = freq_index // (edge_len // 2)
    col_freq = freq_index % (edge_len // 2)
    phase_turns = jnp.mod(row_freq[None, :] * shift_offsets[:, 0:1] + col_freq[None, :] * shift_offsets[:, 1:2], edge_len)
    angles = phase_turns.astype(jnp.float32) * (2.0 * jnp.pi / edge_len)
    return jnp.cos(angles), jnp.sin(angles)


def reference(particles, references, slot_class, log_prior, shift_offsets, group_ids, ctf_table, noise_power):
    half_size = L * L // 2
    full_size = 2 * half_size
    inv_noise = 1.0 / noise_power
    cosines, sine_table = phase_tables(shift_offsets, L)
    stacks = references.astype(jnp.float32)
    stack_real = stacks[:, :, :half_size]
    stack_imag = stacks[:, :, half_size:]
    shifted_real = stack_real[:, :, None, :] * cosines[None, None] + stack_imag[:, :, None, :] * sine_table[None, None]
    shifted_imag = stack_imag[:, :, None, :] * cosines[None, None] - stack_real[:, :, None, :] * sine_table[None, None]
    shifted = jnp.concatenate([shifted_real, shifted_imag], axis=3).astype(jnp.bfloat16)
    shifted = lax.optimization_barrier(shifted).astype(jnp.float32).reshape(CLASSES * R * NS, full_size)
    amplitude = (stack_real * stack_real + stack_imag * stack_imag).reshape(CLASSES * R, half_size)
    power_table = ctf_table * ctf_table * inv_noise
    ref_power = jnp.dot(power_table, amplitude.T, precision=lax.Precision.HIGHEST)
    slot_prior = log_prior[slot_class]
    ctf_square = ctf_table * ctf_table
    blocks = particles.reshape(N_GX * N_GY, PART_DEV, L * L)
    group_blocks = group_ids.reshape(N_GX * N_GY, PART_DEV)

    def accumulate(running, inputs):
        moments, group_weights, evidence_sum = running
        pixels, group_rows = inputs
        images = pixels.astype(jnp.float32).reshape(PART_DEV, L, L)
        spectrum = jnp.fft.fft2(images)[:, :, : L // 2] / L
        real_part = jnp.real(spectrum).reshape(PART_DEV, half_size).astype(jnp.float32)
        imag_part = jnp.imag(spectrum).reshape(PART_DEV, half_size).astype(jnp.float32)
        whiten = ctf_table[group_rows] * inv_noise
        weighted = jnp.concatenate([real_part * whiten, imag_part * whiten], axis=1).astype(jnp.bfloat16)
        weighted_wide = weighted.astype(jnp.float32)
        data_power = jnp.sum((real_part * real_part + imag_part * imag_part) * inv_noise, axis=1)
        intersection = jnp.dot(weighted_wide, shifted.T, precision=lax.Precision.HIGHEST)
        own_power = ref_power[group_rows].reshape(PART_DEV, CLASSES, R)
        logits = intersection.reshape(PART_DEV, CLASSES, R, NS) - 0.5 * own_power[:, :, :, None]
        logits = logits - 0.5 * data_power[:, None, None, None] + slot_prior[None, :, None, None]
        logits = logits.reshape(PART_DEV, CLASSES, R * NS)
        row_max = jnp.max(logits, axis=(1, 2), keepdims=True)
        raised = jnp.exp(logits - row_max)
        normaliser = jnp.sum(raised, axis=(1, 2), keepdims=True)
        weights = raised / normaliser
        evidence = row_max[:, 0, 0] + jnp.log(normaliser[:, 0, 0])
        weights_low = weights.astype(jnp.bfloat16).astype(jnp.float32).reshape(PART_DEV, CLASSES * R * NS)
        moments = moments + jnp.dot(weights_low.T, weighted_wide, precision=lax.Precision.HIGHEST)
        group_hot = (group_rows[:, None] == jnp.arange(G, dtype=jnp.int32)[None, :]).astype(jnp.float32)
        group_weights = group_weights + jnp.dot(jnp.sum(weights, axis=2).T, group_hot, precision=lax.Precision.HIGHEST)
        evidence_sum = evidence_sum + jnp.sum(evidence)
        return (moments, group_weights, evidence_sum), None

    start = (jnp.zeros((CLASSES * R * NS, full_size), jnp.float32), jnp.zeros((CLASSES, G), jnp.float32), jnp.zeros((), jnp.float32))
    (moments, group_weights, evidence_sum), unused = lax.scan(accumulate, start, (blocks, group_blocks))
    moments = moments.reshape(CLASSES, R, NS, full_size)
    moment_real = moments[..., :half_size]
    moment_imag = moments[..., half_size:]
    back_real = jnp.sum(moment_real * cosines[None, None] - moment_imag * sine_table[None, None], axis=2)
    back_imag = jnp.sum(moment_imag * cosines[None, None] + moment_real * sine_table[None, None], axis=2)
    class_sums = jnp.concatenate([back_real, back_imag], axis=2)
    ctf_power = jnp.dot(group_weights, ctf_square, precision=lax.Precision.HIGHEST)
    log_evidence = evidence_sum / (PARTICLES * half_size)
    return (class_sums, ctf_power, log_evidence)
```

```python
import functools
import math

import jax
import jax.numpy as jnp
import numpy as np
from jax import lax
from jax.experimental import pallas as pl
from jax.experimental.pallas import tpu as pltpu
from jax.sharding import PartitionSpec as P

F32 = jnp.float32
BF16 = jnp.bfloat16
LANES = 128
SLOT = 16
FIXED = 6


def dft_tables(side):
    half = side // 2
    fold = LANES // half
    outer = side // fold
    per_row = LANES // side
    y_hi, parity, x = np.meshgrid(np.arange(fold), np.arange(per_row), np.arange(side), indexing="ij")
    y_hi, parity, x = y_hi.reshape(-1, 1), parity.reshape(-1, 1), x.reshape(-1, 1)
    out_par, part, u_lo, v = np.meshgrid(
        np.arange(per_row), np.arange(2), np.arange(fold), np.arange(half), indexing="ij"
    )
    out_par, part, u_lo, v = (t.reshape(1, -1) for t in (out_par, part, u_lo, v))
    turns = (v * x + outer * u_lo * y_hi) % side
    angle = 2.0 * np.pi * turns / side
    table = np.where(part == 0, np.cos(angle), -np.sin(angle)) / side
    table = np.where(parity == out_par, table, 0.0).astype(np.float32)
    high = table.astype(BF16)
    low = (table - high.astype(np.float32)).astype(BF16)
    lane_u = np.arange(LANES) // half
    turn = (np.arange(outer)[:, None] * lane_u[None, :]) % side
    angle = 2.0 * np.pi * turn / side
    twiddle = np.stack([np.cos(angle), np.sin(angle)], 1).astype(np.float32)
    turn = 2.0 * np.pi * np.arange(side) / side
    wave = np.concatenate([np.cos(turn), np.sin(turn)]).astype(np.float32)
    return high, low, twiddle.reshape(2 * outer, LANES), np.tile(wave[None], (8, 1))


def butterflies(real, imag):
    count = len(real)
    if count == 1:
        return real, imag
    even_r, even_i = butterflies(real[0::2], imag[0::2])
    odd_r, odd_i = butterflies(real[1::2], imag[1::2])
    top_r, top_i, low_r, low_i = [], [], [], []
    for k in range(count // 2):
        c = math.cos(2.0 * math.pi * k / count)
        s = math.sin(2.0 * math.pi * k / count)
        r, i = odd_r[k], odd_i[k]
        if k == 0:
            tr, ti = r, i
        elif 4 * k == count:
            tr, ti = i, -r
        elif 8 * k == count:
            tr, ti = (r + i) * c, (i - r) * c
        elif 8 * k == 3 * count:
            tr, ti = (i - r) * s, -(r + i) * s
        else:
            tr, ti = r * c + i * s, i * c - r * s
        top_r.append(even_r[k] + tr)
        top_i.append(even_i[k] + ti)
        low_r.append(even_r[k] - tr)
        low_i.append(even_i[k] - ti)
    return top_r + low_r, top_i + low_i


def split(value):
    high = value.astype(BF16)
    return high, (value - high.astype(F32)).astype(BF16)


def spectra_body(
    ids, images, high, low, twiddle, wave, offsets, ctf, noise,
    rotated, square_high, square_low, power_high, power_low, data_power,
    stacked, partial, rows, w_real, w_imag, cosine, sine, inverse, total,
):
    count, pixels = images.shape
    side = math.isqrt(pixels)
    half = side // 2
    fold = LANES // half
    outer = side // fold
    per_row = LANES // side
    groups = outer // per_row
    shifts = offsets.shape[0]
    columns = noise.shape[1] // LANES
    width = noise.shape[1]

    for m in range(groups):
        for y in range(fold):
            source = (m + groups * y) * LANES
            stacked[m * count:(m + 1) * count, y * LANES:(y + 1) * LANES] = images[:, source:source + LANES]
    partial[...] = jnp.dot(stacked[...], high[...], preferred_element_type=F32)
    partial[...] += jnp.dot(stacked[...], low[...], preferred_element_type=F32)

    inverse[...] = 1.0 / noise[...]

    def fetch(p, carry):
        rows[pl.ds(p, 1), :] = ctf[pl.ds(ids[p], 1), :]
        return carry

    lax.fori_loop(0, count, fetch, 0, unroll=8)

    lane = lax.broadcasted_iota(jnp.int32, (shifts, LANES), 1)
    step_u = offsets[:, 0:1]
    step_v = offsets[:, 1:2]
    for column in range(columns):
        u = lane // half + fold * column
        turn = (u * step_u + (lane % half) * step_v) & (side - 1)
        at = slice(column * LANES, (column + 1) * LANES)
        cosine[:, at] = jnp.take_along_axis(wave[...], turn, axis=1)
        sine[:, at] = jnp.take_along_axis(wave[...], turn + side, axis=1)

    def transform(block, carry):
        base = block * 8
        real, imag = [], []
        for y in range(outer):
            m, parity = y // per_row, y % per_row
            row = pl.ds(m * count + base, 8)
            r = partial[row, (2 * parity) * LANES:(2 * parity + 1) * LANES]
            i = partial[row, (2 * parity + 1) * LANES:(2 * parity + 2) * LANES]
            if y:
                c = twiddle[2 * y:2 * y + 1, :]
                s = twiddle[2 * y + 1:2 * y + 2, :]
                r, i = r * c + i * s, i * c - r * s
            real.append(r)
            imag.append(i)
        real, imag = butterflies(real, imag)
        here = pl.ds(base, 8)
        energy = jnp.zeros((8, LANES), F32)
        for column in range(columns):
            at = slice(column * LANES, (column + 1) * LANES)
            inv = inverse[:, at]
            whiten = rows[here, at] * inv
            r, i = real[column], imag[column]
            energy += (r * r + i * i) * inv
            w_real[here, at] = (r * whiten).astype(BF16).astype(F32)
            w_imag[here, at] = (i * whiten).astype(BF16).astype(F32)
        total[here, :] = energy
        return carry

    lax.fori_loop(0, count // 8, transform, 0)
    data_power[...] = jnp.broadcast_to(jnp.sum(total[...], axis=1, keepdims=True), data_power.shape)

    def rotate(column, carry):
        at = pl.ds(pl.multiple_of(column * LANES, LANES), LANES)
        far = pl.ds(pl.multiple_of(width + column * LANES, LANES), LANES)
        c0 = rows[:, at]
        sq = c0 * c0
        square_high[:, at], square_low[:, at] = split(sq)
        power_high[:, at], power_low[:, at] = split(sq * inverse[:, at])
        wr, wi = w_real[:, at], w_imag[:, at]
        for s in range(shifts):
            c, n = cosine[s:s + 1, at], sine[s:s + 1, at]
            rotated[s * count:(s + 1) * count, at] = (wr * c - wi * n).astype(BF16)
            rotated[s * count:(s + 1) * count, far] = (wi * c + wr * n).astype(BF16)
        return carry

    lax.fori_loop(0, columns, rotate, 0)


def spectra(group_ids, particles, shift_offsets, ctf_table, noise_power):
    count, pixels = particles.shape
    side = math.isqrt(pixels)
    width = noise_power.shape[0]
    shifts = shift_offsets.shape[0]
    high, low, twiddle, wave = dft_tables(side)
    vmem = pl.BlockSpec(memory_space=pltpu.VMEM)
    shape = jax.ShapeDtypeStruct
    plane = shape((count, width), BF16)
    k = high.shape[0]
    groups = pixels // k
    return pl.pallas_call(
        spectra_body,
        out_shape=(shape((shifts * count, 2 * width), BF16), plane, plane, plane, plane, shape((count, LANES), F32)),
        in_specs=[pl.BlockSpec(memory_space=pltpu.SMEM)] + [vmem] * 8,
        out_specs=(vmem,) * 6,
        scratch_shapes=[
            pltpu.VMEM((groups * count, k), BF16),
            pltpu.VMEM((groups * count, high.shape[1]), F32),
            pltpu.VMEM((count, width), F32),
            pltpu.VMEM((count, width), F32),
            pltpu.VMEM((count, width), F32),
            pltpu.VMEM((shifts, width), F32),
            pltpu.VMEM((shifts, width), F32),
            pltpu.VMEM((1, width), F32),
            pltpu.VMEM((count, LANES), F32),
        ],
        name="spectra",
    )(
        group_ids, particles, jnp.asarray(high), jnp.asarray(low), jnp.asarray(twiddle), jnp.asarray(wave),
        shift_offsets, ctf_table, noise_power.reshape(1, width),
    )


def dot_rows(a, b):
    return lax.dot_general(a, b, (((1,), (1,)), ((), ())), preferred_element_type=F32)


def dot_columns(a, b):
    return lax.dot_general(a, b, (((0,), (0,)), ((), ())), preferred_element_type=F32)


def classes_body(digit_bits, classes, *refs):
    others = classes - 1
    place, slots, priors = refs[:3]
    rotated, square_high, square_low, power_high, power_low, data_power, own = refs[3:10]
    mine = refs[10:10 + others]
    theirs = refs[10 + others:10 + 2 * others]
    keep, send, stack, soft, sums, extra = refs[10 + 2 * others:]
    rotations = own.shape[1]
    count = data_power.shape[0]
    shifts = rotated.shape[0] // count
    width = power_high.shape[1]
    lanes = classes * SLOT
    g, h = place[0], place[1]

    here = pl.ds(pl.multiple_of(h * width, width), width)
    there = pl.ds(pl.multiple_of((1 - h) * width, width), width)
    stack[...] = jnp.zeros_like(stack)
    stack[0:rotations, :] = own[0]
    for d in range(1, classes):
        rows = slice(d * SLOT, d * SLOT + rotations)
        stack[rows, here] = mine[d - 1][...]
        stack[rows, there] = theirs[d - 1][...]

    real, imag = stack[:, :width].astype(F32), stack[:, width:].astype(F32)
    amp_high, amp_low = split(real * real + imag * imag)
    own_power = (
        dot_rows(power_high[...], amp_high) + dot_rows(power_high[...], amp_low) + dot_rows(power_low[...], amp_high)
    )
    lane = lax.broadcasted_iota(jnp.int32, (1, lanes), 1)
    prior = jnp.zeros((1, lanes), F32)
    for d in range(classes):
        slot = lax.rem(g - d + classes, classes)
        prior = jnp.where(lane // SLOT == d, priors[slots[slot]], prior)
    prior = jnp.where(lane % SLOT < rotations, prior, -1e30)
    inter = dot_rows(rotated[...], stack[...])
    logits = []
    top = None
    for s in range(shifts):
        l = inter[s * count:(s + 1) * count] - 0.5 * own_power
        l = (l - 0.5 * data_power[:, 0:1]) + prior
        logits.append(l)
        top = l if top is None else jnp.maximum(top, l)
    row_max = jnp.max(top, axis=1, keepdims=True)
    raised = [jnp.exp(l - row_max) for l in logits]
    norm = jnp.sum(functools.reduce(jnp.add, raised), axis=1, keepdims=True)
    weight = jnp.zeros((count, lanes), F32)
    for s in range(shifts):
        w = raised[s] / norm
        weight += w
        soft[s * count:(s + 1) * count, :] = w.astype(BF16)
    evidence = jnp.sum(row_max + jnp.log(norm), axis=0, keepdims=True)

    sums[...] = dot_columns(soft[...], rotated[...])

    wide = lax.broadcasted_iota(jnp.int32, (count, LANES), 1)
    by_class = jnp.zeros((count, LANES), F32)
    for d in range(classes):
        part = jnp.sum(jnp.where(lane // SLOT == d, weight, 0.0), axis=1, keepdims=True)
        by_class = jnp.where(wide == d, part, by_class)
    class_high, class_low = split(by_class)
    extra[...] = (
        dot_columns(class_high, square_high[...])
        + dot_columns(class_high, square_low[...])
        + dot_columns(class_low, square_high[...])
    )

    column = lax.broadcasted_iota(jnp.int32, (1, width), 1)
    number = jnp.round(jnp.broadcast_to(evidence, (1, width)) * float(2**FIXED)).astype(jnp.int32)
    digit = lax.shift_right_logical(jnp.abs(number), jnp.minimum(column * digit_bits, 31))
    digit = jnp.where(column * digit_bits < 31, digit & (2**digit_bits - 1), 0)
    digit = jnp.where(number < 0, -digit, digit).astype(F32)

    empty = jnp.zeros((SLOT - rotations - 2, width), F32)
    for d in range(classes):
        rows = slice(d * SLOT, d * SLOT + rotations)
        tail = jnp.concatenate([extra[d:d + 1, :], digit, empty], axis=0)
        keep[d, 0:rotations, :] = sums[rows, here]
        keep[d, rotations:SLOT, :] = tail
        send[d, :, :] = jnp.concatenate([sums[rows, there], tail], axis=0).astype(BF16)


def classes_call(place, slot_class, log_prior, spectra_out, own, mine, theirs, digit_bits):
    classes = len(mine) + 1
    rotated, *_, data_power = spectra_out
    rows, full = rotated.shape
    width = full // 2
    lanes = classes * SLOT
    vmem = pl.BlockSpec(memory_space=pltpu.VMEM)
    smem = pl.BlockSpec(memory_space=pltpu.SMEM)
    shape = jax.ShapeDtypeStruct
    return pl.pallas_call(
        functools.partial(classes_body, digit_bits, classes),
        out_shape=(shape((classes, SLOT, width), F32), shape((classes, SLOT, width), BF16)),
        in_specs=[smem] * 3 + [vmem] * (7 + 2 * len(mine)),
        out_specs=(vmem, vmem),
        scratch_shapes=[
            pltpu.VMEM((lanes, full), BF16),
            pltpu.VMEM((rows, lanes), BF16),
            pltpu.VMEM((lanes, full), F32),
            pltpu.VMEM((LANES, width), F32),
        ],
        name="classes",
    )(place, slot_class, log_prior, *spectra_out, own, *mine, *theirs)


def tree(parts):
    while len(parts) > 1:
        middle = len(parts) // 2
        parts = [parts[j] + parts[j + middle] for j in range(middle)]
    return parts[0]


def shards(
    particles, references, slot_class, log_prior, shift_offsets, group_ids, ctf_table, noise_power
):
    rings = lax.axis_size("gx")
    spread = lax.axis_size("gy")
    chips = spread // 2
    count = particles.shape[0]
    width = noise_power.shape[0]
    rotations = references.shape[1]
    g = lax.axis_index("gx")
    q = lax.axis_index("gy")
    digit_bits = max(1, 8 - (rings * spread - 1).bit_length())

    def parity(number):
        return bin(number).count("1") & 1

    chip = q // 2
    h = (q & 1) ^ (g & 1)
    for bit in range((chips - 1).bit_length()):
        h = h ^ ((chip >> bit) & 1)

    def move(value, rule):
        pairs = []
        for z in range(rings):
            for c in range(chips):
                for core in range(2):
                    z2, c2, core2 = rule(z, c, core)
                    pairs.append((z * spread + 2 * c + core, z2 * spread + 2 * c2 + core2))
        return lax.ppermute(value, ("gx", "gy"), pairs)

    def shift(d):
        return lambda z, c, core: ((z + d) % rings, c, core ^ (d & 1))

    def swap(z, c, core):
        return z, c, core ^ 1

    def hop(bit):
        return lambda z, c, core: (z, c ^ (1 << bit), core ^ 1)

    half_stack = lax.dynamic_slice_in_dim(references[0], h * width, width, 1)
    mine = [move(half_stack, shift(d)) for d in range(1, rings)]
    theirs = [move(value, swap) for value in mine]
    spectra_out = spectra(group_ids, particles, shift_offsets, ctf_table, noise_power)
    place = jnp.stack([g, h]).astype(jnp.int32)
    keep, send = classes_call(place, slot_class, log_prior, spectra_out, references, mine, theirs, digit_bits)

    pair = keep + move(send, swap).astype(F32)
    gathered = [pair[0]]
    for d in range(1, rings):
        gathered.append(move(pair[d].astype(BF16), shift(rings - d)).astype(F32))
    owned = tree(gathered)
    for bit in range((chips - 1).bit_length()):
        low = owned.astype(BF16)
        owned = lax.reduce_precision(owned, 8, 7) + move(low, hop(bit)).astype(F32)

    other = move(owned, swap)
    first = jnp.where(h == 0, owned, other)
    second = jnp.where(h == 0, other, owned)
    class_sums = jnp.concatenate([first[:rotations], second[:rotations]], axis=1)[None]
    ctf_power = first[rotations][None]
    scale = np.zeros((LANES,), np.float64)
    for j in range(-(-31 // digit_bits)):
        scale[j] = 2.0 ** (j * digit_bits - FIXED)
    scale = scale / (count * rings * spread * width)
    log_evidence = jnp.sum(first[rotations + 1, :LANES] * jnp.asarray(scale, F32))
    return class_sums, ctf_power, log_evidence


def solution(mesh):
    return jax.shard_map(
        shards,
        mesh=mesh,
        in_specs=(
            P(("gx", "gy"), None),
            P("gx", None, None),
            P(),
            P(),
            P(),
            P(("gx", "gy")),
            P(),
            P(),
        ),
        out_specs=(P("gx", None, None), P("gx", None), P()),
        check_vma=False,
    )
```

```python
import functools
import math

import jax
import jax.numpy as jnp
import numpy as np
from jax import lax
from jax.experimental import pallas as pl
from jax.experimental.pallas import tpu as pltpu
from jax.sharding import PartitionSpec as P

F32 = jnp.float32
BF16 = jnp.bfloat16
LANES = 128
SLOT = 16
FIXED = 6


def dft_tables(side):
    half = side // 2
    fold = LANES // half
    outer = side // fold
    per_row = LANES // side
    y_hi, parity, x = np.meshgrid(np.arange(fold), np.arange(per_row), np.arange(side), indexing="ij")
    y_hi, parity, x = y_hi.reshape(-1, 1), parity.reshape(-1, 1), x.reshape(-1, 1)
    out_par, part, u_lo, v = np.meshgrid(
        np.arange(per_row), np.arange(2), np.arange(fold), np.arange(half), indexing="ij"
    )
    out_par, part, u_lo, v = (t.reshape(1, -1) for t in (out_par, part, u_lo, v))
    turns = (v * x + outer * u_lo * y_hi) % side
    angle = 2.0 * np.pi * turns / side
    table = np.where(part == 0, np.cos(angle), -np.sin(angle)) / side
    table = np.where(parity == out_par, table, 0.0).astype(np.float32)
    high = table.astype(BF16)
    low = (table - high.astype(np.float32)).astype(BF16)
    lane_u = np.arange(LANES) // half
    turn = (np.arange(outer)[:, None] * lane_u[None, :]) % side
    angle = 2.0 * np.pi * turn / side
    twiddle = np.stack([np.cos(angle), np.sin(angle)], 1).astype(np.float32)
    turn = 2.0 * np.pi * np.arange(side) / side
    wave = np.concatenate([np.cos(turn), np.sin(turn)]).astype(np.float32)
    return high, low, twiddle.reshape(2 * outer, LANES), np.tile(wave[None], (8, 1))


def butterflies(real, imag):
    count = len(real)
    if count == 1:
        return real, imag
    even_r, even_i = butterflies(real[0::2], imag[0::2])
    odd_r, odd_i = butterflies(real[1::2], imag[1::2])
    top_r, top_i, low_r, low_i = [], [], [], []
    for k in range(count // 2):
        c = math.cos(2.0 * math.pi * k / count)
        s = math.sin(2.0 * math.pi * k / count)
        r, i = odd_r[k], odd_i[k]
        if k == 0:
            tr, ti = r, i
        elif 4 * k == count:
            tr, ti = i, -r
        elif 8 * k == count:
            tr, ti = (r + i) * c, (i - r) * c
        elif 8 * k == 3 * count:
            tr, ti = (i - r) * s, -(r + i) * s
        else:
            tr, ti = r * c + i * s, i * c - r * s
        top_r.append(even_r[k] + tr)
        top_i.append(even_i[k] + ti)
        low_r.append(even_r[k] - tr)
        low_i.append(even_i[k] - ti)
    return top_r + low_r, top_i + low_i


def split(value):
    high = value.astype(BF16)
    return high, (value - high.astype(F32)).astype(BF16)


def spectra_body(
    ids_far, images_far, high_far, low_far, twiddle_far, wave_far, offsets_far, ctf_far, noise_far,
    rotated, square_high, square_low, power_high, power_low, data_power,
    ids, images, high, low, twiddle, wave, offsets, ctf, noise,
    stacked, partial, rows, w_real, w_imag, cosine, sine, inverse, total, arrived,
):
    copies = [
        pltpu.make_async_copy(far, near, arrived.at[j])
        for j, (far, near) in enumerate((
            (images_far, images), (high_far, high), (low_far, low), (offsets_far, offsets), (wave_far, wave),
            (noise_far, noise), (ids_far, ids), (ctf_far, ctf), (twiddle_far, twiddle),
        ))
    ]
    for copy in copies:
        copy.start()
    count, pixels = images.shape
    side = math.isqrt(pixels)
    half = side // 2
    fold = LANES // half
    outer = side // fold
    per_row = LANES // side
    groups = outer // per_row
    shifts = offsets.shape[1]
    columns = noise.shape[1] // LANES
    width = noise.shape[1]

    for copy in copies[:6]:
        copy.wait()
    for m in range(groups):
        for y in range(fold):
            source = (m + groups * y) * LANES
            stacked[m * count:(m + 1) * count, y * LANES:(y + 1) * LANES] = images[:, source:source + LANES]
    partial[...] = jnp.dot(stacked[...], high[...], preferred_element_type=F32)
    partial[...] += jnp.dot(stacked[...], low[...], preferred_element_type=F32)

    inverse[...] = 1.0 / noise[...]
    for copy in copies[6:]:
        copy.wait()

    def fetch(p, carry):
        rows[pl.ds(p, 1), :] = ctf[pl.ds(ids[p], 1), :]
        return carry

    lax.fori_loop(0, count, fetch, 0, unroll=8)

    lane = lax.broadcasted_iota(jnp.int32, (shifts, LANES), 1)
    shift = lax.broadcasted_iota(jnp.int32, (shifts, LANES), 0)
    step_u = jnp.zeros((shifts, LANES), jnp.int32)
    step_v = jnp.zeros((shifts, LANES), jnp.int32)
    for s in range(shifts):
        step_u = jnp.where(shift == s, offsets[0, s], step_u)
        step_v = jnp.where(shift == s, offsets[1, s], step_v)
    for column in range(columns):
        u = lane // half + fold * column
        turn = (u * step_u + (lane % half) * step_v) & (side - 1)
        at = slice(column * LANES, (column + 1) * LANES)
        cosine[:, at] = jnp.take_along_axis(wave[...], turn, axis=1)
        sine[:, at] = jnp.take_along_axis(wave[...], turn + side, axis=1)

    def transform(block, carry):
        base = block * 8
        real, imag = [], []
        for y in range(outer):
            m, parity = y // per_row, y % per_row
            row = pl.ds(m * count + base, 8)
            r = partial[row, (2 * parity) * LANES:(2 * parity + 1) * LANES]
            i = partial[row, (2 * parity + 1) * LANES:(2 * parity + 2) * LANES]
            if y:
                c = twiddle[2 * y:2 * y + 1, :]
                s = twiddle[2 * y + 1:2 * y + 2, :]
                r, i = r * c + i * s, i * c - r * s
            real.append(r)
            imag.append(i)
        real, imag = butterflies(real, imag)
        here = pl.ds(base, 8)
        energy = jnp.zeros((8, LANES), F32)
        for column in range(columns):
            at = slice(column * LANES, (column + 1) * LANES)
            inv = inverse[:, at]
            whiten = rows[here, at] * inv
            r, i = real[column], imag[column]
            energy += (r * r + i * i) * inv
            w_real[here, at] = (r * whiten).astype(BF16).astype(F32)
            w_imag[here, at] = (i * whiten).astype(BF16).astype(F32)
        total[here, :] = energy
        return carry

    lax.fori_loop(0, count // 8, transform, 0)
    data_power[...] = jnp.broadcast_to(jnp.sum(total[...], axis=1, keepdims=True), data_power.shape)

    def rotate(column, carry):
        at = pl.ds(pl.multiple_of(column * LANES, LANES), LANES)
        far = pl.ds(pl.multiple_of(width + column * LANES, LANES), LANES)
        c0 = rows[:, at]
        sq = c0 * c0
        square_high[:, at], square_low[:, at] = split(sq)
        power_high[:, at], power_low[:, at] = split(sq * inverse[:, at])
        wr, wi = w_real[:, at], w_imag[:, at]
        for s in range(shifts):
            c, n = cosine[s:s + 1, at], sine[s:s + 1, at]
            rotated[s * count:(s + 1) * count, at] = (wr * c - wi * n).astype(BF16)
            rotated[s * count:(s + 1) * count, far] = (wi * c + wr * n).astype(BF16)
        return carry

    lax.fori_loop(0, columns, rotate, 0)


def spectra(group_ids, particles, shift_offsets, ctf_table, noise_power):
    count, pixels = particles.shape
    side = math.isqrt(pixels)
    width = noise_power.shape[0]
    shifts = shift_offsets.shape[0]
    high, low, twiddle, wave = dft_tables(side)
    vmem = pl.BlockSpec(memory_space=pltpu.VMEM)
    far = pl.BlockSpec(memory_space=pltpu.HBM)
    shape = pltpu.VMEM
    plane = shape((count, width), BF16)
    k = high.shape[0]
    groups = pixels // k
    return pl.pallas_call(
        spectra_body,
        out_shape=(shape((shifts * count, 2 * width), BF16), plane, plane, plane, plane, shape((count, LANES), F32)),
        cost_estimate=pl.CostEstimate(flops=2**32, transcendentals=0, bytes_accessed=2**23),
        in_specs=[far] * 9,
        out_specs=(vmem,) * 6,
        scratch_shapes=[
            pltpu.SMEM(group_ids.shape, jnp.int32),
            pltpu.VMEM(particles.shape, particles.dtype),
            pltpu.VMEM(high.shape, BF16),
            pltpu.VMEM(low.shape, BF16),
            pltpu.VMEM(twiddle.shape, F32),
            pltpu.VMEM(wave.shape, F32),
            pltpu.SMEM(shift_offsets.shape[::-1], jnp.int32),
            pltpu.VMEM(ctf_table.shape, F32),
            pltpu.VMEM((1, width), F32),
            pltpu.VMEM((groups * count, k), BF16),
            pltpu.VMEM((groups * count, high.shape[1]), F32),
            pltpu.VMEM((count, width), F32),
            pltpu.VMEM((count, width), F32),
            pltpu.VMEM((count, width), F32),
            pltpu.VMEM((shifts, width), F32),
            pltpu.VMEM((shifts, width), F32),
            pltpu.VMEM((1, width), F32),
            pltpu.VMEM((count, LANES), F32),
            pltpu.SemaphoreType.DMA((9,)),
        ],
        compiler_params=pltpu.CompilerParams(vmem_limit_bytes=24 * 2**20),
        name="spectra",
    )(*(
        pltpu.with_memory_space_constraint(x, pltpu.HBM)
        for x in (
            group_ids, particles, jnp.asarray(high), jnp.asarray(low), jnp.asarray(twiddle), jnp.asarray(wave),
            shift_offsets.T, ctf_table, noise_power.reshape(1, width),
        )
    ))


def dot_rows(a, b):
    return lax.dot_general(a, b, (((1,), (1,)), ((), ())), preferred_element_type=F32)


def dot_columns(a, b):
    return lax.dot_general(a, b, (((0,), (0,)), ((), ())), preferred_element_type=F32)


def classes_body(digit_bits, classes, *refs):
    others = classes - 1
    ring, side, slots, priors = refs[:4]
    rotated, square_high, square_low, power_high, power_low, data_power, own = refs[4:11]
    mine = refs[11:11 + others]
    theirs = refs[11 + others:11 + 2 * others]
    keep, send, stack, soft, sums, extra = refs[11 + 2 * others:]
    rotations = own.shape[1]
    count = data_power.shape[0]
    shifts = rotated.shape[0] // count
    width = power_high.shape[1]
    lanes = classes * SLOT
    g, h = ring[0], side[0]

    here = pl.ds(pl.multiple_of(h * width, width), width)
    there = pl.ds(pl.multiple_of((1 - h) * width, width), width)
    stack[...] = jnp.zeros_like(stack)
    stack[0:rotations, :] = own[0]
    for d in range(1, classes):
        rows = slice(d * SLOT, d * SLOT + rotations)
        stack[rows, here] = mine[d - 1][...]
        stack[rows, there] = theirs[d - 1][...]

    real, imag = stack[:, :width].astype(F32), stack[:, width:].astype(F32)
    amp_high, amp_low = split(real * real + imag * imag)
    own_power = (
        dot_rows(power_high[...], amp_high) + dot_rows(power_high[...], amp_low) + dot_rows(power_low[...], amp_high)
    )
    lane = lax.broadcasted_iota(jnp.int32, (1, lanes), 1)
    prior = jnp.zeros((1, lanes), F32)
    for d in range(classes):
        slot = lax.rem(g - d + classes, classes)
        prior = jnp.where(lane // SLOT == d, priors[slots[slot]], prior)
    prior = jnp.where(lane % SLOT < rotations, prior, -1e30)
    inter = dot_rows(rotated[...], stack[...])
    logits = []
    top = None
    for s in range(shifts):
        l = inter[s * count:(s + 1) * count] - 0.5 * own_power
        l = (l - 0.5 * data_power[:, 0:1]) + prior
        logits.append(l)
        top = l if top is None else jnp.maximum(top, l)
    row_max = jnp.max(top, axis=1, keepdims=True)
    raised = [jnp.exp(l - row_max) for l in logits]
    norm = jnp.sum(functools.reduce(jnp.add, raised), axis=1, keepdims=True)
    weight = jnp.zeros((count, lanes), F32)
    for s in range(shifts):
        w = raised[s] / norm
        weight += w
        soft[s * count:(s + 1) * count, :] = w.astype(BF16)
    evidence = jnp.sum(row_max + jnp.log(norm), axis=0, keepdims=True)

    sums[...] = dot_columns(soft[...], rotated[...])

    wide = lax.broadcasted_iota(jnp.int32, (count, LANES), 1)
    by_class = jnp.zeros((count, LANES), F32)
    for d in range(classes):
        part = jnp.sum(jnp.where(lane // SLOT == d, weight, 0.0), axis=1, keepdims=True)
        by_class = jnp.where(wide == d, part, by_class)
    class_high, class_low = split(by_class)
    extra[...] = (
        dot_columns(class_high, square_high[...])
        + dot_columns(class_high, square_low[...])
        + dot_columns(class_low, square_high[...])
    )

    column = lax.broadcasted_iota(jnp.int32, (1, width), 1)
    number = jnp.round(jnp.broadcast_to(evidence, (1, width)) * float(2**FIXED)).astype(jnp.int32)
    digit = lax.shift_right_logical(jnp.abs(number), jnp.minimum(column * digit_bits, 31))
    digit = jnp.where(column * digit_bits < 31, digit & (2**digit_bits - 1), 0)
    digit = jnp.where(number < 0, -digit, digit).astype(F32)

    empty = jnp.zeros((SLOT - rotations - 2, width), F32)
    for d in range(classes):
        rows = slice(d * SLOT, d * SLOT + rotations)
        tail = jnp.concatenate([extra[d:d + 1, :], digit, empty], axis=0)
        keep[d, 0:rotations, :] = sums[rows, here]
        keep[d, rotations:SLOT, :] = tail
        send[d, :, :] = jnp.concatenate([sums[rows, there], tail], axis=0).astype(BF16)


def classes_call(ring, side, slot_class, log_prior, spectra_out, own, mine, theirs, digit_bits):
    classes = len(mine) + 1
    rotated, *_, data_power = spectra_out
    rows, full = rotated.shape
    width = full // 2
    lanes = classes * SLOT
    vmem = pl.BlockSpec(memory_space=pltpu.VMEM)
    smem = pl.BlockSpec(memory_space=pltpu.SMEM)
    shape = pltpu.VMEM
    spectra_out = [pltpu.with_memory_space_constraint(x, pltpu.VMEM) for x in spectra_out]
    return pl.pallas_call(
        functools.partial(classes_body, digit_bits, classes),
        out_shape=(shape((classes, SLOT, width), F32), shape((classes, SLOT, width), BF16)),
        in_specs=[smem] * 4 + [vmem] * (7 + 2 * len(mine)),
        out_specs=(vmem, vmem),
        scratch_shapes=[
            pltpu.VMEM((lanes, full), BF16),
            pltpu.VMEM((rows, lanes), BF16),
            pltpu.VMEM((lanes, full), F32),
            pltpu.VMEM((LANES, width), F32),
        ],
        compiler_params=pltpu.CompilerParams(vmem_limit_bytes=24 * 2**20),
        name="classes",
    )(ring, side, slot_class, log_prior, *spectra_out, own, *mine, *theirs)


def finish_body(side, owned, other, scale, sums, ctf_power, log_evidence):
    rotations, _, full = sums.shape
    width = full // 2
    h = side[0]
    here = pl.ds(pl.multiple_of(h * width, width), width)
    there = pl.ds(pl.multiple_of((1 - h) * width, width), width)
    sums[:, 0, here] = owned[:rotations, :]
    sums[:, 0, there] = other[:rotations, :]
    tail = jnp.where(h == 0, owned[rotations:, :], other[rotations:, :])
    ctf_power[...] = tail[0:1, :]
    log_evidence[...] = jnp.sum(tail[1:2, :LANES] * scale[...], axis=1, keepdims=True)


def finish(side, owned, other, rotations, scale):
    width = owned.shape[1]
    vmem = pl.BlockSpec(memory_space=pltpu.VMEM)
    shape = jax.ShapeDtypeStruct
    return pl.pallas_call(
        finish_body,
        out_shape=(shape((rotations, 1, 2 * width), F32), shape((1, width), F32), shape((1, 1), F32)),
        in_specs=[pl.BlockSpec(memory_space=pltpu.SMEM)] + [vmem] * 3,
        out_specs=(vmem,) * 3,
        compiler_params=pltpu.CompilerParams(vmem_limit_bytes=8 * 2**20),
        name="finish",
    )(side, owned, other, scale)


def tree(parts):
    while len(parts) > 1:
        middle = len(parts) // 2
        parts = [parts[j] + parts[j + middle] for j in range(middle)]
    return parts[0]


def shards(
    particles, references, slot_class, log_prior, shift_offsets, group_ids, ctf_table, noise_power
):
    rings = lax.axis_size("gx")
    spread = lax.axis_size("gy")
    chips = spread // 2
    count = particles.shape[0]
    width = noise_power.shape[0]
    rotations = references.shape[1]
    g = lax.axis_index("gx")
    q = lax.axis_index("gy")
    digit_bits = max(1, 8 - (rings * spread - 1).bit_length())

    def parity(number):
        return bin(number).count("1") & 1

    chip = q // 2
    h = (q & 1) ^ (g & 1)
    for bit in range((chips - 1).bit_length()):
        h = h ^ ((chip >> bit) & 1)

    def move(value, rule):
        pairs = []
        for z in range(rings):
            for c in range(chips):
                for core in range(2):
                    z2, c2, core2 = rule(z, c, core)
                    pairs.append((z * spread + 2 * c + core, z2 * spread + 2 * c2 + core2))
        return lax.ppermute(value, ("gx", "gy"), pairs)

    def shift(d):
        return lambda z, c, core: ((z + d) % rings, c, core ^ (d & 1))

    def swap(z, c, core):
        return z, c, core ^ 1

    def hop(bit):
        return lambda z, c, core: (z, c ^ (1 << bit), core ^ 1)

    half_stack = lax.dynamic_slice_in_dim(references[0], h * width, width, 1)
    mine = [move(half_stack, shift(d)) for d in range(1, rings)]
    spectra_out = spectra(group_ids, particles, shift_offsets, ctf_table, noise_power)
    mine, spectra_out = lax.optimization_barrier((mine, spectra_out))
    theirs = [move(value, swap) for value in mine]
    ring, side = g.reshape(1), h.reshape(1)
    keep, send = classes_call(ring, side, slot_class, log_prior, spectra_out, references, mine, theirs, digit_bits)

    pair = keep + move(send, swap).astype(F32)
    gathered = [pair[0]]
    for d in range(1, rings):
        gathered.append(move(pair[d].astype(BF16), shift(rings - d)).astype(F32))
    owned = tree(gathered)
    for bit in range((chips - 1).bit_length()):
        low = owned.astype(BF16)
        owned = lax.reduce_precision(owned, 8, 7) + move(low, hop(bit)).astype(F32)

    other = move(owned, swap)
    scale = np.zeros((1, LANES), np.float64)
    for j in range(-(-31 // digit_bits)):
        scale[0, j] = 2.0 ** (j * digit_bits - FIXED)
    scale = scale / (count * rings * spread * width)
    sums, ctf_power, log_evidence = finish(side, owned, other, rotations, jnp.asarray(scale, F32))
    return sums.reshape(1, rotations, 2 * width), ctf_power, log_evidence.reshape(())


def solution(mesh):
    return jax.shard_map(
        shards,
        mesh=mesh,
        in_specs=(
            P(("gx", "gy"), None),
            P("gx", None, None),
            P(),
            P(),
            P(),
            P(("gx", "gy")),
            P(),
            P(),
        ),
        out_specs=(P("gx", None, None), P("gx", None), P()),
        check_vma=False,
    )
```

```python
import functools
import math

import jax
import jax.numpy as jnp
import numpy as np
from jax import lax
from jax.experimental import pallas as pl
from jax.experimental.pallas import tpu as pltpu
from jax.sharding import PartitionSpec as P

F32 = jnp.float32
BF16 = jnp.bfloat16
LANES = 128
TOP = 8
FIXED = 6


def dft_tables(side):
    half = side // 2
    fold = LANES // half
    outer = side // fold
    per_row = LANES // side
    y_hi, parity, x = np.meshgrid(np.arange(fold), np.arange(per_row), np.arange(side), indexing="ij")
    y_hi, parity, x = y_hi.reshape(-1, 1), parity.reshape(-1, 1), x.reshape(-1, 1)
    out_par, part, u_lo, v = np.meshgrid(
        np.arange(per_row), np.arange(2), np.arange(fold), np.arange(half), indexing="ij"
    )
    out_par, part, u_lo, v = (t.reshape(1, -1) for t in (out_par, part, u_lo, v))
    turns = (v * x + outer * u_lo * y_hi) % side
    angle = 2.0 * np.pi * turns / side
    table = np.where(part == 0, np.cos(angle), -np.sin(angle)) / side
    table = np.where(parity == out_par, table, 0.0).astype(np.float32)
    high = table.astype(BF16)
    low = (table - high.astype(np.float32)).astype(BF16)
    lane_u = np.arange(LANES) // half
    turn = (np.arange(outer)[:, None] * lane_u[None, :]) % side
    angle = 2.0 * np.pi * turn / side
    twiddle = np.stack([np.cos(angle), np.sin(angle)], 1).astype(np.float32)
    turn = 2.0 * np.pi * np.arange(side) / side
    wave = np.concatenate([np.cos(turn), np.sin(turn)]).astype(np.float32)
    return high, low, twiddle.reshape(2 * outer, LANES), np.tile(wave[None], (8, 1))


def butterflies(real, imag):
    count = len(real)
    if count == 1:
        return real, imag
    even_r, even_i = butterflies(real[0::2], imag[0::2])
    odd_r, odd_i = butterflies(real[1::2], imag[1::2])
    top_r, top_i, low_r, low_i = [], [], [], []
    for k in range(count // 2):
        c = math.cos(2.0 * math.pi * k / count)
        s = math.sin(2.0 * math.pi * k / count)
        r, i = odd_r[k], odd_i[k]
        if k == 0:
            tr, ti = r, i
        elif 4 * k == count:
            tr, ti = i, -r
        elif 8 * k == count:
            tr, ti = (r + i) * c, (i - r) * c
        elif 8 * k == 3 * count:
            tr, ti = (i - r) * s, -(r + i) * s
        else:
            tr, ti = r * c + i * s, i * c - r * s
        top_r.append(even_r[k] + tr)
        top_i.append(even_i[k] + ti)
        low_r.append(even_r[k] - tr)
        low_i.append(even_i[k] - ti)
    return top_r + low_r, top_i + low_i


def split(value):
    high = value.astype(BF16)
    return high, (value - high.astype(F32)).astype(BF16)


def spectra_body(
    ids_far, images_far, high_far, low_far, twiddle_far, wave_far, offsets_far, ctf_far, noise_far,
    rotated, squares, powers, data_power,
    ids, images, high, low, twiddle, wave, offsets, ctf, noise,
    stacked, partial, rows, w_real, w_imag, cosine, sine, inverse, total, arrived,
):
    copies = [
        pltpu.make_async_copy(far, near, arrived.at[j])
        for j, (far, near) in enumerate((
            (images_far, images), (high_far, high), (low_far, low), (offsets_far, offsets), (wave_far, wave),
            (noise_far, noise), (ids_far, ids), (ctf_far, ctf), (twiddle_far, twiddle),
        ))
    ]
    for copy in copies:
        copy.start()
    count, pixels = images.shape
    side = math.isqrt(pixels)
    half = side // 2
    fold = LANES // half
    outer = side // fold
    per_row = LANES // side
    groups = outer // per_row
    shifts = offsets.shape[1]
    columns = noise.shape[1] // LANES
    width = noise.shape[1]

    for copy in copies[:6]:
        copy.wait()
    for m in range(groups):
        for y in range(fold):
            source = (m + groups * y) * LANES
            stacked[m * count:(m + 1) * count, y * LANES:(y + 1) * LANES] = images[:, source:source + LANES]
    partial[...] = jnp.dot(stacked[...], high[...], preferred_element_type=F32)
    partial[...] += jnp.dot(stacked[...], low[...], preferred_element_type=F32)

    inverse[...] = 1.0 / noise[...]
    for copy in copies[6:]:
        copy.wait()

    def fetch(p, carry):
        rows[pl.ds(p, 1), :] = ctf[pl.ds(ids[p], 1), :]
        return carry

    lax.fori_loop(0, count, fetch, 0, unroll=8)

    lane = lax.broadcasted_iota(jnp.int32, (shifts, LANES), 1)
    shift = lax.broadcasted_iota(jnp.int32, (shifts, LANES), 0)
    step_u = jnp.zeros((shifts, LANES), jnp.int32)
    step_v = jnp.zeros((shifts, LANES), jnp.int32)
    for s in range(shifts):
        step_u = jnp.where(shift == s, offsets[0, s], step_u)
        step_v = jnp.where(shift == s, offsets[1, s], step_v)
    for column in range(columns):
        u = lane // half + fold * column
        turn = (u * step_u + (lane % half) * step_v) & (side - 1)
        at = slice(column * LANES, (column + 1) * LANES)
        cosine[:, at] = jnp.take_along_axis(wave[...], turn, axis=1)
        sine[:, at] = jnp.take_along_axis(wave[...], turn + side, axis=1)

    def transform(block, carry):
        base = block * 8
        real, imag = [], []
        for y in range(outer):
            m, parity = y // per_row, y % per_row
            row = pl.ds(m * count + base, 8)
            r = partial[row, (2 * parity) * LANES:(2 * parity + 1) * LANES]
            i = partial[row, (2 * parity + 1) * LANES:(2 * parity + 2) * LANES]
            if y:
                c = twiddle[2 * y:2 * y + 1, :]
                s = twiddle[2 * y + 1:2 * y + 2, :]
                r, i = r * c + i * s, i * c - r * s
            real.append(r)
            imag.append(i)
        real, imag = butterflies(real, imag)
        here = pl.ds(base, 8)
        energy = jnp.zeros((8, LANES), F32)
        for column in range(columns):
            at = slice(column * LANES, (column + 1) * LANES)
            inv = inverse[:, at]
            whiten = rows[here, at] * inv
            r, i = real[column], imag[column]
            energy += (r * r + i * i) * inv
            w_real[here, at] = (r * whiten).astype(BF16).astype(F32)
            w_imag[here, at] = (i * whiten).astype(BF16).astype(F32)
        total[here, :] = energy
        return carry

    lax.fori_loop(0, count // 8, transform, 0)
    energy = jnp.sum(jnp.transpose(total[...]), axis=0, keepdims=True)
    data_power[...] = jnp.concatenate([energy] * (data_power.shape[1] // count), axis=1)

    def rotate(column, carry):
        at = pl.ds(pl.multiple_of(column * LANES, LANES), LANES)
        square = rows[:, at] * rows[:, at]
        high, low = split(square)
        squares[column, 0:count, :] = high
        squares[column, count:, :] = low
        high, low = split(square * inverse[:, at])
        powers[column, 0:count, :] = high
        powers[column, count:, :] = low
        wr, wi = w_real[:, at], w_imag[:, at]
        for s in range(shifts):
            c, n = cosine[s:s + 1, at], sine[s:s + 1, at]
            rotated[column, s * count:(s + 1) * count, :] = (wr * c - wi * n).astype(BF16)
            rotated[columns + column, s * count:(s + 1) * count, :] = (wi * c + wr * n).astype(BF16)
        return carry

    lax.fori_loop(0, columns, rotate, 0)


def spectra(group_ids, particles, shift_offsets, ctf_table, noise_power):
    count, pixels = particles.shape
    side = math.isqrt(pixels)
    width = noise_power.shape[0]
    shifts = shift_offsets.shape[0]
    high, low, twiddle, wave = dft_tables(side)
    vmem = pl.BlockSpec(memory_space=pltpu.VMEM)
    far = pl.BlockSpec(memory_space=pltpu.HBM)
    shape = pltpu.VMEM
    columns = width // LANES
    plane = shape((columns, 2 * count, LANES), BF16)
    k = high.shape[0]
    groups = pixels // k
    return pl.pallas_call(
        spectra_body,
        out_shape=(shape((2 * columns, shifts * count, LANES), BF16), plane, plane, shape((1, 2 * count), F32)),
        cost_estimate=pl.CostEstimate(flops=2**32, transcendentals=0, bytes_accessed=2**23),
        in_specs=[far] * 9,
        out_specs=(vmem,) * 4,
        scratch_shapes=[
            pltpu.SMEM(group_ids.shape, jnp.int32),
            pltpu.VMEM(particles.shape, particles.dtype),
            pltpu.VMEM(high.shape, BF16),
            pltpu.VMEM(low.shape, BF16),
            pltpu.VMEM(twiddle.shape, F32),
            pltpu.VMEM(wave.shape, F32),
            pltpu.SMEM(shift_offsets.shape[::-1], jnp.int32),
            pltpu.VMEM(ctf_table.shape, F32),
            pltpu.VMEM((1, width), F32),
            pltpu.VMEM((groups * count, k), BF16),
            pltpu.VMEM((groups * count, high.shape[1]), F32),
            pltpu.VMEM((count, width), F32),
            pltpu.VMEM((count, width), F32),
            pltpu.VMEM((count, width), F32),
            pltpu.VMEM((shifts, width), F32),
            pltpu.VMEM((shifts, width), F32),
            pltpu.VMEM((1, width), F32),
            pltpu.VMEM((count, LANES), F32),
            pltpu.SemaphoreType.DMA((9,)),
        ],
        compiler_params=pltpu.CompilerParams(vmem_limit_bytes=24 * 2**20),
        name="spectra",
    )(*(
        pltpu.with_memory_space_constraint(x, pltpu.HBM)
        for x in (
            group_ids, particles, jnp.asarray(high), jnp.asarray(low), jnp.asarray(twiddle), jnp.asarray(wave),
            shift_offsets.T, ctf_table, noise_power.reshape(1, width),
        )
    ))


def dot_rows(a, b):
    return lax.dot_general(a, b, (((1,), (1,)), ((), ())), preferred_element_type=F32)


def side_by_side(planes, first, count):
    return jnp.concatenate([planes[first + j] for j in range(count)], axis=1)


def fold(value):
    rest = value.shape[0] - TOP
    pieces = TOP // rest
    step = value.shape[1] // pieces
    tail = jnp.concatenate([value[TOP:, j * step:(j + 1) * step] for j in range(pieces)], axis=0)
    return jnp.concatenate([value[:TOP], tail], axis=1)


def folded_width(rotations, width):
    return width + (rotations - TOP) * width // TOP


def pack_body(side, far, mine, theirs, near, arrived):
    width = near.shape[2]
    h = side[0]
    copies = []
    for j, half in enumerate((h, 1 - h)):
        source = far.at[0, :, pl.ds(pl.multiple_of(half * width, width), width)]
        copies.append(pltpu.make_async_copy(source, near.at[j], arrived.at[j]))
    for copy in copies:
        copy.start()
    for j, out in enumerate((mine, theirs)):
        copies[j].wait()
        out[...] = fold(near[j].astype(F32)).astype(BF16)


def pack(side, references):
    _, rotations, full = references.shape
    width = full // 2
    vmem = pl.BlockSpec(memory_space=pltpu.VMEM)
    out = pltpu.VMEM((TOP, folded_width(rotations, width)), BF16)
    return pl.pallas_call(
        pack_body,
        out_shape=(out, out),
        in_specs=[pl.BlockSpec(memory_space=pltpu.SMEM), pl.BlockSpec(memory_space=pltpu.HBM)],
        out_specs=(vmem, vmem),
        scratch_shapes=[pltpu.VMEM((2, rotations, width), BF16), pltpu.SemaphoreType.DMA((2,))],
        compiler_params=pltpu.CompilerParams(vmem_limit_bytes=4 * 2**20),
        name="pack",
    )(side, pltpu.with_memory_space_constraint(references, pltpu.HBM))


def half_scores(h, rotated, powers, packed, stack):
    classes = len(packed)
    rows, width = stack.shape
    rest = rows // classes - TOP
    pieces = TOP // rest
    step = width // pieces
    for d, ref in enumerate(packed):
        value = ref[...].astype(F32)
        stack[d * TOP:(d + 1) * TOP, :] = value[:, :width]
        low = classes * TOP + d * rest
        for j in range(pieces):
            stack[low:low + rest, j * step:(j + 1) * step] = value[j * rest:(j + 1) * rest, width:]
    planes = width // LANES
    value = stack[...]
    inter = dot_rows(value.astype(BF16), side_by_side(rotated, h * planes, planes))
    high, low = split(value * value)
    power = dot_rows(jnp.concatenate([high, low], axis=0), side_by_side(powers, 0, planes))
    power = power[:rows] + power[rows:]
    power = 0.5 * (power + pltpu.roll(power, power.shape[1] // 2, axis=1))
    return [inter[:, j:j + LANES] - power for j in range(0, inter.shape[1], LANES)]


def first_body(side, rotated, powers, *refs):
    *packed, scores, stack = refs
    parts = half_scores(side[0], rotated, powers, packed, stack)
    for j, part in enumerate(parts):
        scores[:, j * LANES:(j + 1) * LANES] = part


def half_sums(half, soft, by_class, digits, rotated, squares, out):
    classes = out.shape[0]
    rows = soft.shape[0]
    rest = rows // classes - TOP
    planes = rotated.shape[0] // 2
    width = planes * LANES
    pieces = TOP // rest
    step = width // pieces
    sums = jnp.dot(soft, side_by_side(rotated, half * planes, planes), preferred_element_type=F32)
    narrow = planes // 2
    extra = jnp.dot(by_class, side_by_side(squares, half * narrow, narrow), preferred_element_type=F32)
    extra = extra[:classes] + extra[extra.shape[0] // 2:extra.shape[0] // 2 + classes]
    at = width + step
    for d in range(classes):
        out[d, :, 0:width] = sums[d * TOP:(d + 1) * TOP, :].astype(out.dtype)
        low = sums[classes * TOP + d * rest:classes * TOP + (d + 1) * rest, :]
        tail = jnp.concatenate([low[:, j * step:(j + 1) * step] for j in range(pieces)], axis=0)
        out[d, :, width:at] = tail.astype(out.dtype)
        lines = extra[d:d + 1, :]
        tall = jnp.concatenate([lines[:, j * LANES:(j + 1) * LANES] for j in range(narrow)], axis=0)
        out[d, :, at:at + LANES] = tall.astype(out.dtype)
        out[d, :, at + LANES:at + 2 * LANES] = digits.astype(out.dtype)


def second_body(digit_bits, ring, side, slots, priors, *refs):
    rotated, powers, squares, data_power, scores = refs[:5]
    *packed, send, soft_out, class_out, digits_out, stack = refs[5:]
    classes = len(packed)
    rows = scores.shape[0]
    rest = rows // classes - TOP
    count = powers.shape[1] // 2
    there = 1 - side[0]
    parts = half_scores(there, rotated, powers, packed, stack)

    line = lax.broadcasted_iota(jnp.int32, (rows, LANES), 0)
    owner = jnp.where(line < classes * TOP, line // TOP, (line - classes * TOP) // rest)
    prior = jnp.zeros((rows, LANES), F32)
    for d in range(classes):
        slot = lax.rem(ring[0] - d + classes, classes)
        prior = jnp.where(owner == d, priors[slots[slot]], prior)
    energy = 0.5 * data_power[...]
    logits = [
        ((scores[:, j * LANES:(j + 1) * LANES] + part) - energy) + prior for j, part in enumerate(parts)
    ]
    top = jnp.max(functools.reduce(jnp.maximum, logits), axis=0, keepdims=True)
    top = jnp.maximum(top, pltpu.roll(top, count, axis=1))
    raised = [jnp.exp(l - top) for l in logits]
    norm = jnp.sum(functools.reduce(jnp.add, raised), axis=0, keepdims=True)
    norm = norm + pltpu.roll(norm, count, axis=1)
    scale = 1.0 / norm
    weights = [r * scale for r in raised]
    soft = jnp.concatenate([w.astype(BF16) for w in weights], axis=1)
    soft_out[...] = soft

    weight = functools.reduce(jnp.add, weights)
    weight = weight + pltpu.roll(weight, count, axis=1)
    base = classes * TOP
    per_class = jnp.concatenate(
        [
            jnp.sum(weight[d * TOP:(d + 1) * TOP], axis=0, keepdims=True)
            + jnp.sum(weight[base + d * rest:base + (d + 1) * rest], axis=0, keepdims=True)
            for d in range(classes)
        ]
        + [jnp.zeros((-classes % 8, LANES), F32)] * (1 if classes % 8 else 0),
        axis=0,
    )
    high = per_class.astype(BF16).astype(F32)
    lane = lax.broadcasted_iota(jnp.int32, per_class.shape, 1)
    by_class = jnp.concatenate([high, jnp.where(lane < count, per_class - high, 0.0)], axis=0).astype(BF16)
    class_out[...] = by_class

    lane = lax.broadcasted_iota(jnp.int32, (1, LANES), 1)
    evidence = jnp.sum(jnp.where(lane < count, top + jnp.log(norm), 0.0), axis=1, keepdims=True)
    number = jnp.round(jnp.broadcast_to(evidence, (1, LANES)) * float(2**FIXED)).astype(jnp.int32)
    digit = lax.shift_right_logical(jnp.abs(number), jnp.minimum(lane * digit_bits, 31))
    digit = jnp.where(lane * digit_bits < 31, digit & (2**digit_bits - 1), 0)
    digit = jnp.where(number < 0, -digit, digit).astype(F32)
    digits = jnp.broadcast_to(digit, (TOP, LANES))
    digits_out[...] = digits
    half_sums(there, soft, by_class, digits, rotated, squares, send)


def third_body(side, rotated, squares, soft, by_class, digits, keep):
    half_sums(side[0], soft[...], by_class[...], digits[...], rotated, squares, keep)


def local_call(body, out_shape, smem, vmem, scratch, name):
    chip = pl.BlockSpec(memory_space=pltpu.VMEM)
    return pl.pallas_call(
        body,
        out_shape=out_shape,
        in_specs=[pl.BlockSpec(memory_space=pltpu.SMEM)] * len(smem) + [chip] * len(vmem),
        out_specs=jax.tree.map(lambda _: chip, out_shape, is_leaf=lambda x: not isinstance(x, tuple)),
        scratch_shapes=scratch,
        compiler_params=pltpu.CompilerParams(vmem_limit_bytes=16 * 2**20),
        cost_estimate=pl.CostEstimate(flops=2**31, transcendentals=0, bytes_accessed=2**21),
        name=name,
    )(*smem, *(pltpu.with_memory_space_constraint(x, pltpu.VMEM) for x in vmem))


def finish_body(side, owned, other, scale, sums, ctf_power, log_evidence):
    rotations, _, full = sums.shape
    width = full // 2
    rest = rotations - TOP
    pieces = TOP // rest
    step = width // pieces
    at = width + step
    narrow = width // 2
    for half, source in ((side[0], owned), (1 - side[0], other)):
        sums[0:TOP, 0, pl.ds(pl.multiple_of(half * width, width), width)] = source[:, :width]
        for j in range(pieces):
            here = pl.ds(pl.multiple_of(half * width + j * step, step), step)
            sums[TOP:, 0, here] = source[j * rest:(j + 1) * rest, width:at]
        for j in range(narrow // LANES):
            here = pl.ds(pl.multiple_of(half * narrow + j * LANES, LANES), LANES)
            ctf_power[:, here] = source[j:j + 1, at:at + LANES]
    log_evidence[...] = jnp.sum(owned[0:1, at + LANES:at + 2 * LANES] * scale[...], axis=1, keepdims=True)


def finish(side, owned, other, rotations, width, scale):
    vmem = pl.BlockSpec(memory_space=pltpu.VMEM)
    shape = jax.ShapeDtypeStruct
    return pl.pallas_call(
        finish_body,
        out_shape=(shape((rotations, 1, 2 * width), F32), shape((1, width), F32), shape((1, 1), F32)),
        in_specs=[pl.BlockSpec(memory_space=pltpu.SMEM)] + [vmem] * 3,
        out_specs=(vmem,) * 3,
        compiler_params=pltpu.CompilerParams(vmem_limit_bytes=8 * 2**20),
        name="finish",
    )(side, owned, other, scale)


def tree(parts):
    while len(parts) > 1:
        middle = len(parts) // 2
        parts = [parts[j] + parts[j + middle] for j in range(middle)]
    return parts[0]


def shards(
    particles, references, slot_class, log_prior, shift_offsets, group_ids, ctf_table, noise_power
):
    rings = lax.axis_size("gx")
    spread = lax.axis_size("gy")
    chips = spread // 2
    count = particles.shape[0]
    width = noise_power.shape[0]
    rotations = references.shape[1]
    g = lax.axis_index("gx")
    q = lax.axis_index("gy")
    digit_bits = max(1, 8 - (rings * spread - 1).bit_length())

    def parity(number):
        return bin(number).count("1") & 1

    chip = q // 2
    h = (q & 1) ^ (g & 1)
    for bit in range((chips - 1).bit_length()):
        h = h ^ ((chip >> bit) & 1)

    def move(value, rule):
        pairs = []
        for z in range(rings):
            for c in range(chips):
                for core in range(2):
                    z2, c2, core2 = rule(z, c, core)
                    pairs.append((z * spread + 2 * c + core, z2 * spread + 2 * c2 + core2))
        return lax.ppermute(value, ("gx", "gy"), pairs)

    def shift(d):
        return lambda z, c, core: ((z + d) % rings, c, core ^ (d & 1))

    def swap(z, c, core):
        return z, c, core ^ 1

    def hop(bit):
        return lambda z, c, core: (z, c ^ (1 << bit), core ^ 1)

    ring, side = g.reshape(1), h.reshape(1)
    near, far = pack(side, references)
    mine = [move(near, shift(d)) for d in range(1, rings)]
    rotated, squares, powers, data_power = spectra(group_ids, particles, shift_offsets, ctf_table, noise_power)
    mine, near, far, rotated, squares, powers, data_power = lax.optimization_barrier(
        (mine, near, far, rotated, squares, powers, data_power)
    )
    theirs = [move(value, swap) for value in mine]
    rows = rings * rotations
    planes = rotated.shape[1]
    stack = pltpu.VMEM((rows, width), F32)
    scores = local_call(
        first_body, pltpu.VMEM((rows, planes), F32), (side,), (rotated, powers, near, *mine), [stack], "first"
    )
    theirs, scores = lax.optimization_barrier((theirs, scores))
    block = (rings, TOP, folded_width(rotations, width) + 2 * LANES)
    send, soft, by_class, digits = local_call(
        functools.partial(second_body, digit_bits),
        (
            pltpu.VMEM(block, BF16),
            pltpu.VMEM((rows, planes), BF16),
            pltpu.VMEM((2 * (rings + -rings % 8), LANES), BF16),
            pltpu.VMEM((TOP, LANES), F32),
        ),
        (ring, side, slot_class, log_prior),
        (rotated, powers, squares, data_power, scores, far, *theirs),
        [stack],
        "second",
    )
    arrived = move(send, swap)
    keep = local_call(
        third_body, pltpu.VMEM(block, F32), (side,), (rotated, squares, soft, by_class, digits), [], "third"
    )
    arrived, keep = lax.optimization_barrier((arrived, keep))
    pair = keep + arrived.astype(F32)
    gathered = [pair[0]]
    for d in range(1, rings):
        gathered.append(move(pair[d].astype(BF16), shift(rings - d)).astype(F32))
    owned = tree(gathered)
    for bit in range((chips - 1).bit_length()):
        low = owned.astype(BF16)
        owned = lax.reduce_precision(owned, 8, 7) + move(low, hop(bit)).astype(F32)

    other = move(owned, swap)
    scale = np.zeros((1, LANES), np.float64)
    for j in range(-(-31 // digit_bits)):
        scale[0, j] = 2.0 ** (j * digit_bits - FIXED)
    scale = scale / (count * rings * spread * width)
    sums, ctf_power, log_evidence = finish(side, owned, other, rotations, width, jnp.asarray(scale, F32))
    return sums.reshape(1, rotations, 2 * width), ctf_power, log_evidence.reshape(())


def solution(mesh):
    return jax.shard_map(
        shards,
        mesh=mesh,
        in_specs=(
            P(("gx", "gy"), None),
            P("gx", None, None),
            P(),
            P(),
            P(),
            P(("gx", "gy")),
            P(),
            P(),
        ),
        out_specs=(P("gx", None, None), P("gx", None), P()),
        check_vma=False,
    )
```

```python
import functools
import math

import jax
import jax.numpy as jnp
import numpy as np
from jax import lax
from jax.experimental import pallas as pl
from jax.experimental.pallas import tpu as pltpu
from jax.sharding import PartitionSpec as P

F32 = jnp.float32
BF16 = jnp.bfloat16
LANES = 128
TOP = 8
FIXED = 6


def own_half():
    place = lax.axis_index("gy")
    half = place & 1
    for bit in range(1, (lax.axis_size("gy") - 1).bit_length()):
        half = half ^ ((place >> bit) & 1)
    return half


def dft_tables(side):
    half = side // 2
    fold = LANES // half
    outer = side // fold
    per_row = LANES // side
    y_hi, parity, x = np.meshgrid(np.arange(fold), np.arange(per_row), np.arange(side), indexing="ij")
    y_hi, parity, x = y_hi.reshape(-1, 1), parity.reshape(-1, 1), x.reshape(-1, 1)
    out_par, part, u_lo, v = np.meshgrid(
        np.arange(per_row), np.arange(2), np.arange(fold), np.arange(half), indexing="ij"
    )
    out_par, part, u_lo, v = (t.reshape(1, -1) for t in (out_par, part, u_lo, v))
    turns = (v * x + outer * u_lo * y_hi) % side
    angle = 2.0 * np.pi * turns / side
    table = np.where(part == 0, np.cos(angle), -np.sin(angle)) / side
    table = np.where(parity == out_par, table, 0.0).astype(np.float32)
    high = table.astype(BF16)
    low = (table - high.astype(np.float32)).astype(BF16)
    lane_u = np.arange(LANES) // half
    turn = (np.arange(outer)[:, None] * lane_u[None, :]) % side
    angle = 2.0 * np.pi * turn / side
    twiddle = np.stack([np.cos(angle), np.sin(angle)], 1).astype(np.float32)
    turn = 2.0 * np.pi * np.arange(side) / side
    wave = np.concatenate([np.cos(turn), np.sin(turn)]).astype(np.float32)
    return high, low, twiddle.reshape(2 * outer, LANES), np.tile(wave[None], (8, 1))


def butterflies(real, imag):
    count = len(real)
    if count == 1:
        return real, imag
    even_r, even_i = butterflies(real[0::2], imag[0::2])
    odd_r, odd_i = butterflies(real[1::2], imag[1::2])
    top_r, top_i, low_r, low_i = [], [], [], []
    for k in range(count // 2):
        c = math.cos(2.0 * math.pi * k / count)
        s = math.sin(2.0 * math.pi * k / count)
        r, i = odd_r[k], odd_i[k]
        if k == 0:
            tr, ti = r, i
        elif 4 * k == count:
            tr, ti = i, -r
        elif 8 * k == count:
            tr, ti = (r + i) * c, (i - r) * c
        elif 8 * k == 3 * count:
            tr, ti = (i - r) * s, -(r + i) * s
        else:
            tr, ti = r * c + i * s, i * c - r * s
        top_r.append(even_r[k] + tr)
        top_i.append(even_i[k] + ti)
        low_r.append(even_r[k] - tr)
        low_i.append(even_i[k] - ti)
    return top_r + low_r, top_i + low_i


def split(value):
    high = value.astype(BF16)
    return high, (value - high.astype(F32)).astype(BF16)


def spectra_body(
    ids_far, images_far, high_far, low_far, twiddle_far, wave_far, offsets_far, ctf_far, noise_far, slots_far, priors_far,
    rotated, squares, powers, data_power, prior,
    ids, images, high, low, twiddle, wave, offsets, ctf, noise, slots, priors,
    stacked, partial, rows, w_real, w_imag, cosine, sine, inverse, total, arrived,
):
    copies = [
        pltpu.make_async_copy(far, near, arrived.at[j])
        for j, (far, near) in enumerate((
            (offsets_far, offsets), (wave_far, wave), (noise_far, noise), (slots_far, slots), (priors_far, priors),
            (images_far, images), (high_far, high), (low_far, low), (ids_far, ids), (ctf_far, ctf), (twiddle_far, twiddle),
        ))
    ]
    for copy in copies:
        copy.start()
    count, pixels = images.shape
    side = math.isqrt(pixels)
    half = side // 2
    fold = LANES // half
    outer = side // fold
    per_row = LANES // side
    groups = outer // per_row
    shifts = offsets.shape[1]
    columns = noise.shape[1] // LANES
    width = noise.shape[1]

    for copy in copies[:5]:
        copy.wait()
    inverse[...] = 1.0 / noise[...]
    lane = lax.broadcasted_iota(jnp.int32, (shifts, LANES), 1)
    shift = lax.broadcasted_iota(jnp.int32, (shifts, LANES), 0)
    step_u = jnp.zeros((shifts, LANES), jnp.int32)
    step_v = jnp.zeros((shifts, LANES), jnp.int32)
    for s in range(shifts):
        step_u = jnp.where(shift == s, offsets[0, s], step_u)
        step_v = jnp.where(shift == s, offsets[1, s], step_v)
    for column in range(columns):
        u = lane // half + fold * column
        turn = (u * step_u + (lane % half) * step_v) & (side - 1)
        at = slice(column * LANES, (column + 1) * LANES)
        cosine[:, at] = jnp.take_along_axis(wave[...], turn, axis=1)
        sine[:, at] = jnp.take_along_axis(wave[...], turn + side, axis=1)

    classes = slots.shape[0]
    scored = prior.shape[0]
    rest = scored // classes - TOP
    line = lax.broadcasted_iota(jnp.int32, prior.shape, 0)
    owner = jnp.where(line < classes * TOP, line // TOP, (line - classes * TOP) // rest)
    ring = lax.axis_index("gx")
    value = jnp.zeros(prior.shape, F32)
    for d in range(classes):
        value = jnp.where(owner == d, priors[slots[lax.rem(ring - d + classes, classes)]], value)
    prior[...] = value

    for copy in copies[5:8]:
        copy.wait()
    for m in range(groups):
        for y in range(fold):
            source = (m + groups * y) * LANES
            stacked[m * count:(m + 1) * count, y * LANES:(y + 1) * LANES] = images[:, source:source + LANES]
    partial[...] = jnp.dot(stacked[...], high[...], preferred_element_type=F32)
    partial[...] += jnp.dot(stacked[...], low[...], preferred_element_type=F32)

    for copy in copies[8:]:
        copy.wait()

    def fetch(p, carry):
        rows[pl.ds(p, 1), :] = ctf[pl.ds(ids[p], 1), :]
        return carry

    lax.fori_loop(0, count, fetch, 0, unroll=16)

    def transform(block, carry):
        base = block * 8
        real, imag = [], []
        for y in range(outer):
            m, parity = y // per_row, y % per_row
            row = pl.ds(m * count + base, 8)
            r = partial[row, (2 * parity) * LANES:(2 * parity + 1) * LANES]
            i = partial[row, (2 * parity + 1) * LANES:(2 * parity + 2) * LANES]
            if y:
                c = twiddle[2 * y:2 * y + 1, :]
                s = twiddle[2 * y + 1:2 * y + 2, :]
                r, i = r * c + i * s, i * c - r * s
            real.append(r)
            imag.append(i)
        real, imag = butterflies(real, imag)
        here = pl.ds(base, 8)
        energy = jnp.zeros((8, LANES), F32)
        for column in range(columns):
            at = slice(column * LANES, (column + 1) * LANES)
            inv = inverse[:, at]
            whiten = rows[here, at] * inv
            r, i = real[column], imag[column]
            energy += (r * r + i * i) * inv
            w_real[here, at] = (r * whiten).astype(BF16).astype(F32)
            w_imag[here, at] = (i * whiten).astype(BF16).astype(F32)
        total[here, :] = energy
        return carry

    lax.fori_loop(0, count // 8, transform, 0)
    energy = jnp.sum(jnp.transpose(total[...]), axis=0, keepdims=True)
    data_power[...] = jnp.concatenate([energy] * (data_power.shape[1] // count), axis=1)

    def rotate(column, carry):
        at = pl.ds(pl.multiple_of(column * LANES, LANES), LANES)
        square = rows[:, at] * rows[:, at]
        high, low = split(square)
        squares[column, 0:count, :] = high
        squares[column, count:, :] = low
        high, low = split(square * inverse[:, at])
        powers[column, 0:count, :] = high
        powers[column, count:, :] = low
        wr, wi = w_real[:, at], w_imag[:, at]
        for s in range(shifts):
            c, n = cosine[s:s + 1, at], sine[s:s + 1, at]
            rotated[column, s * count:(s + 1) * count, :] = (wr * c - wi * n).astype(BF16)
            rotated[columns + column, s * count:(s + 1) * count, :] = (wi * c + wr * n).astype(BF16)
        return carry

    lax.fori_loop(0, columns, rotate, 0)


def spectra(group_ids, particles, shift_offsets, ctf_table, noise_power, slot_class, log_prior, rotations):
    count, pixels = particles.shape
    side = math.isqrt(pixels)
    width = noise_power.shape[0]
    shifts = shift_offsets.shape[0]
    high, low, twiddle, wave = dft_tables(side)
    vmem = pl.BlockSpec(memory_space=pltpu.VMEM)
    far = pl.BlockSpec(memory_space=pltpu.HBM)
    shape = pltpu.VMEM
    columns = width // LANES
    plane = shape((columns, 2 * count, LANES), BF16)
    scored = shape((slot_class.shape[0] * rotations, LANES), F32)
    k = high.shape[0]
    groups = pixels // k
    return pl.pallas_call(
        spectra_body,
        out_shape=(shape((2 * columns, shifts * count, LANES), BF16), plane, plane, shape((1, 2 * count), F32), scored),
        cost_estimate=pl.CostEstimate(flops=2**32, transcendentals=0, bytes_accessed=2**23),
        in_specs=[far] * 11,
        out_specs=(vmem,) * 5,
        scratch_shapes=[
            pltpu.SMEM(group_ids.shape, jnp.int32),
            pltpu.VMEM(particles.shape, particles.dtype),
            pltpu.VMEM(high.shape, BF16),
            pltpu.VMEM(low.shape, BF16),
            pltpu.VMEM(twiddle.shape, F32),
            pltpu.VMEM(wave.shape, F32),
            pltpu.SMEM(shift_offsets.shape[::-1], jnp.int32),
            pltpu.VMEM(ctf_table.shape, F32),
            pltpu.VMEM((1, width), F32),
            pltpu.SMEM(slot_class.shape, jnp.int32),
            pltpu.SMEM(log_prior.shape, F32),
            pltpu.VMEM((groups * count, k), BF16),
            pltpu.VMEM((groups * count, high.shape[1]), F32),
            pltpu.VMEM((count, width), F32),
            pltpu.VMEM((count, width), F32),
            pltpu.VMEM((count, width), F32),
            pltpu.VMEM((shifts, width), F32),
            pltpu.VMEM((shifts, width), F32),
            pltpu.VMEM((1, width), F32),
            pltpu.VMEM((count, LANES), F32),
            pltpu.SemaphoreType.DMA((11,)),
        ],
        compiler_params=pltpu.CompilerParams(vmem_limit_bytes=24 * 2**20),
        name="spectra",
    )(*(
        pltpu.with_memory_space_constraint(x, pltpu.HBM)
        for x in (
            group_ids, particles, jnp.asarray(high), jnp.asarray(low), jnp.asarray(twiddle), jnp.asarray(wave),
            shift_offsets.T, ctf_table, noise_power.reshape(1, width), slot_class, log_prior,
        )
    ))


def dot_rows(a, b):
    return lax.dot_general(a, b, (((1,), (1,)), ((), ())), preferred_element_type=F32)


def side_by_side(planes, first, count):
    return jnp.concatenate([planes[first + j] for j in range(count)], axis=1)


def fold(value):
    rest = value.shape[0] - TOP
    pieces = TOP // rest
    step = value.shape[1] // pieces
    tail = jnp.concatenate([value[TOP:, j * step:(j + 1) * step] for j in range(pieces)], axis=0)
    return jnp.concatenate([value[:TOP], tail], axis=1)


def folded_width(rotations, width):
    return width + (rotations - TOP) * width // TOP


def pack_body(far, mine, theirs, near, arrived):
    width = near.shape[2]
    h = own_half()
    copies = []
    for j, half in enumerate((h, 1 - h)):
        source = far.at[0, :, pl.ds(pl.multiple_of(half * width, width), width)]
        copies.append(pltpu.make_async_copy(source, near.at[j], arrived.at[j]))
    for copy in copies:
        copy.start()
    for j, out in enumerate((mine, theirs)):
        copies[j].wait()
        out[...] = fold(near[j].astype(F32)).astype(BF16)


def pack(references):
    _, rotations, full = references.shape
    width = full // 2
    vmem = pl.BlockSpec(memory_space=pltpu.VMEM)
    out = pltpu.VMEM((TOP, folded_width(rotations, width)), BF16)
    return pl.pallas_call(
        pack_body,
        out_shape=(out, out),
        in_specs=[pl.BlockSpec(memory_space=pltpu.HBM)],
        out_specs=(vmem, vmem),
        scratch_shapes=[pltpu.VMEM((2, rotations, width), BF16), pltpu.SemaphoreType.DMA((2,))],
        compiler_params=pltpu.CompilerParams(vmem_limit_bytes=4 * 2**20),
        name="pack",
    )(pltpu.with_memory_space_constraint(references, pltpu.HBM))


def half_scores(h, rotated, powers, packed, stack):
    classes = len(packed)
    rows, width = stack.shape
    rest = rows // classes - TOP
    pieces = TOP // rest
    step = width // pieces
    for d, ref in enumerate(packed):
        value = ref[...].astype(F32)
        stack[d * TOP:(d + 1) * TOP, :] = value[:, :width]
        low = classes * TOP + d * rest
        for j in range(pieces):
            stack[low:low + rest, j * step:(j + 1) * step] = value[j * rest:(j + 1) * rest, width:]
    planes = width // LANES
    value = stack[...]
    inter = dot_rows(value.astype(BF16), side_by_side(rotated, h * planes, planes))
    high, low = split(value * value)
    power = dot_rows(jnp.concatenate([high, low], axis=0), side_by_side(powers, 0, planes))
    power = power[:rows] + power[rows:]
    power = 0.5 * (power + pltpu.roll(power, power.shape[1] // 2, axis=1))
    return [inter[:, j:j + LANES] - power for j in range(0, inter.shape[1], LANES)]


def first_body(rotated, powers, *refs):
    *packed, scores, stack = refs
    parts = half_scores(own_half(), rotated, powers, packed, stack)
    for j, part in enumerate(parts):
        scores[:, j * LANES:(j + 1) * LANES] = part


def half_sums(half, soft, by_class, digits, rotated, squares, out):
    classes = out.shape[0]
    rows = soft.shape[0]
    rest = rows // classes - TOP
    planes = rotated.shape[0] // 2
    width = planes * LANES
    pieces = TOP // rest
    step = width // pieces
    sums = jnp.dot(soft, side_by_side(rotated, half * planes, planes), preferred_element_type=F32)
    narrow = planes // 2
    extra = jnp.dot(by_class, side_by_side(squares, half * narrow, narrow), preferred_element_type=F32)
    extra = extra[:classes] + extra[extra.shape[0] // 2:extra.shape[0] // 2 + classes]
    at = width + step
    for d in range(classes):
        out[d, :, 0:width] = sums[d * TOP:(d + 1) * TOP, :].astype(out.dtype)
        low = sums[classes * TOP + d * rest:classes * TOP + (d + 1) * rest, :]
        tail = jnp.concatenate([low[:, j * step:(j + 1) * step] for j in range(pieces)], axis=0)
        out[d, :, width:at] = tail.astype(out.dtype)
        lines = extra[d:d + 1, :]
        tall = jnp.concatenate([lines[:, j * LANES:(j + 1) * LANES] for j in range(narrow)], axis=0)
        out[d, :, at:at + LANES] = tall.astype(out.dtype)
        out[d, :, at + LANES:at + 2 * LANES] = digits.astype(out.dtype)


def second_body(digit_bits, rotated, powers, squares, data_power, prior, scores, *refs):
    *packed, send, soft_out, class_out, digits_out, stack = refs
    classes = len(packed)
    rows = scores.shape[0]
    rest = rows // classes - TOP
    count = powers.shape[1] // 2
    there = 1 - own_half()
    parts = half_scores(there, rotated, powers, packed, stack)
    energy = 0.5 * data_power[...]
    logits = [
        ((scores[:, j * LANES:(j + 1) * LANES] + part) - energy) + prior[...] for j, part in enumerate(parts)
    ]
    top = jnp.max(functools.reduce(jnp.maximum, logits), axis=0, keepdims=True)
    top = jnp.maximum(top, pltpu.roll(top, count, axis=1))
    raised = [jnp.exp(l - top) for l in logits]
    norm = jnp.sum(functools.reduce(jnp.add, raised), axis=0, keepdims=True)
    norm = norm + pltpu.roll(norm, count, axis=1)
    scale = 1.0 / norm
    weights = [r * scale for r in raised]
    soft = jnp.concatenate([w.astype(BF16) for w in weights], axis=1)
    soft_out[...] = soft

    weight = functools.reduce(jnp.add, weights)
    weight = weight + pltpu.roll(weight, count, axis=1)
    base = classes * TOP
    per_class = jnp.concatenate(
        [
            jnp.sum(weight[d * TOP:(d + 1) * TOP], axis=0, keepdims=True)
            + jnp.sum(weight[base + d * rest:base + (d + 1) * rest], axis=0, keepdims=True)
            for d in range(classes)
        ]
        + [jnp.zeros((-classes % 8, LANES), F32)] * (1 if classes % 8 else 0),
        axis=0,
    )
    high = per_class.astype(BF16).astype(F32)
    lane = lax.broadcasted_iota(jnp.int32, per_class.shape, 1)
    by_class = jnp.concatenate([high, jnp.where(lane < count, per_class - high, 0.0)], axis=0).astype(BF16)
    class_out[...] = by_class

    lane = lax.broadcasted_iota(jnp.int32, (1, LANES), 1)
    evidence = jnp.sum(jnp.where(lane < count, top + jnp.log(norm), 0.0), axis=1, keepdims=True)
    number = jnp.round(jnp.broadcast_to(evidence, (1, LANES)) * float(2**FIXED)).astype(jnp.int32)
    digit = lax.shift_right_logical(jnp.abs(number), jnp.minimum(lane * digit_bits, 31))
    digit = jnp.where(lane * digit_bits < 31, digit & (2**digit_bits - 1), 0)
    digit = jnp.where(number < 0, -digit, digit).astype(F32)
    digits = jnp.broadcast_to(digit, (TOP, LANES))
    digits_out[...] = digits
    half_sums(there, soft, by_class, digits, rotated, squares, send)


def third_body(rotated, squares, soft, by_class, digits, keep):
    half_sums(own_half(), soft[...], by_class[...], digits[...], rotated, squares, keep)


def local_call(body, out_shape, operands, scratch, name):
    chip = pl.BlockSpec(memory_space=pltpu.VMEM)
    return pl.pallas_call(
        body,
        out_shape=out_shape,
        in_specs=[chip] * len(operands),
        out_specs=jax.tree.map(lambda _: chip, out_shape, is_leaf=lambda x: not isinstance(x, tuple)),
        scratch_shapes=scratch,
        compiler_params=pltpu.CompilerParams(vmem_limit_bytes=16 * 2**20),
        cost_estimate=pl.CostEstimate(flops=2**31, transcendentals=0, bytes_accessed=2**21),
        name=name,
    )(*(pltpu.with_memory_space_constraint(x, pltpu.VMEM) for x in operands))


def finish_body(owned, other, scale, sums, ctf_power, log_evidence):
    rotations, _, full = sums.shape
    width = full // 2
    rest = rotations - TOP
    pieces = TOP // rest
    step = width // pieces
    at = width + step
    narrow = width // 2
    h = own_half()
    for half, source in ((h, owned), (1 - h, other)):
        sums[0:TOP, 0, pl.ds(pl.multiple_of(half * width, width), width)] = source[:, :width]
        for j in range(pieces):
            here = pl.ds(pl.multiple_of(half * width + j * step, step), step)
            sums[TOP:, 0, here] = source[j * rest:(j + 1) * rest, width:at]
        for j in range(narrow // LANES):
            here = pl.ds(pl.multiple_of(half * narrow + j * LANES, LANES), LANES)
            ctf_power[:, here] = source[j:j + 1, at:at + LANES]
    log_evidence[...] = jnp.sum(owned[0:1, at + LANES:at + 2 * LANES] * scale[...], axis=1, keepdims=True)


def finish(owned, other, rotations, width, scale):
    vmem = pl.BlockSpec(memory_space=pltpu.VMEM)
    shape = jax.ShapeDtypeStruct
    return pl.pallas_call(
        finish_body,
        out_shape=(shape((rotations, 1, 2 * width), F32), shape((1, width), F32), shape((1, 1), F32)),
        in_specs=[vmem] * 3,
        out_specs=(vmem,) * 3,
        compiler_params=pltpu.CompilerParams(vmem_limit_bytes=8 * 2**20),
        name="finish",
    )(owned, other, scale)


def tree(parts):
    while len(parts) > 1:
        middle = len(parts) // 2
        parts = [parts[j] + parts[j + middle] for j in range(middle)]
    return parts[0]


def pairwise(parts):
    while len(parts) > 1:
        parts = [a + b for a, b in zip(parts[0::2], parts[1::2], strict=True)]
    return parts[0]


def shards(
    particles, references, slot_class, log_prior, shift_offsets, group_ids, ctf_table, noise_power
):
    rings = lax.axis_size("gx")
    spread = lax.axis_size("gy")
    chips = spread // 2
    count = particles.shape[0]
    width = noise_power.shape[0]
    rotations = references.shape[1]
    digit_bits = max(1, 8 - (rings * spread - 1).bit_length())

    def move(value, rule):
        pairs = []
        for z in range(rings):
            for c in range(chips):
                for core in range(2):
                    z2, c2, core2 = rule(z, c, core)
                    pairs.append((z * spread + 2 * c + core, z2 * spread + 2 * c2 + core2))
        return lax.ppermute(value, ("gx", "gy"), pairs)

    def shift(d):
        return lambda z, c, core: ((z + d) % rings, c, core)

    def swap(z, c, core):
        return z, c, core ^ 1

    def hop(mask):
        return lambda z, c, core: (z, c ^ mask, core ^ (bin(mask).count("1") & 1))

    near, far = pack(references)
    mine = [move(near, shift(d)) for d in range(1, rings)]
    spectra_out = spectra(
        group_ids, particles, shift_offsets, ctf_table, noise_power, slot_class, log_prior, rotations
    )
    mine, near, far, spectra_out = lax.optimization_barrier((mine, near, far, spectra_out))
    rotated, squares, powers, data_power, prior = spectra_out
    theirs = [move(value, swap) for value in mine]
    rows = rings * rotations
    planes = rotated.shape[1]
    stack = pltpu.VMEM((rows, width), F32)
    scores = local_call(first_body, pltpu.VMEM((rows, planes), F32), (rotated, powers, near, *mine), [stack], "first")
    theirs, scores = lax.optimization_barrier((theirs, scores))
    block = (rings, TOP, folded_width(rotations, width) + 2 * LANES)
    send, soft, by_class, digits = local_call(
        functools.partial(second_body, digit_bits),
        (
            pltpu.VMEM(block, BF16),
            pltpu.VMEM((rows, planes), BF16),
            pltpu.VMEM((2 * (rings + -rings % 8), LANES), BF16),
            pltpu.VMEM((TOP, LANES), F32),
        ),
        (rotated, powers, squares, data_power, prior, scores, far, *theirs),
        [stack],
        "second",
    )
    arrived = move(send, swap)
    keep = local_call(
        third_body, pltpu.VMEM(block, F32), (rotated, squares, soft, by_class, digits), [], "third"
    )
    arrived, keep = lax.optimization_barrier((arrived, keep))
    pair = keep + arrived.astype(F32)
    gathered = [pair[0]]
    for d in range(1, rings):
        gathered.append(move(pair[d].astype(BF16), shift(rings - d)).astype(F32))
    owned = tree(gathered)
    low = owned.astype(BF16)
    parts = [low] + [move(low, hop(mask)) for mask in range(1, chips)]
    owned = pairwise([part.astype(F32) for part in parts])
    other = move(owned, swap)
    scale = np.zeros((1, LANES), np.float64)
    for j in range(-(-31 // digit_bits)):
        scale[0, j] = 2.0 ** (j * digit_bits - FIXED)
    scale = scale / (count * rings * spread * width)
    sums, ctf_power, log_evidence = finish(owned, other, rotations, width, jnp.asarray(scale, F32))
    return sums.reshape(1, rotations, 2 * width), ctf_power, log_evidence.reshape(())


def solution(mesh):
    return jax.shard_map(
        shards,
        mesh=mesh,
        in_specs=(
            P(("gx", "gy"), None),
            P("gx", None, None),
            P(),
            P(),
            P(),
            P(("gx", "gy")),
            P(),
            P(),
        ),
        out_specs=(P("gx", None, None), P("gx", None), P()),
        check_vma=False,
    )
```

```python
import functools
import math

import jax
import jax.numpy as jnp
import numpy as np
from jax import lax
from jax.experimental import pallas as pl
from jax.experimental.pallas import tpu as pltpu
from jax.sharding import PartitionSpec as P

F32 = jnp.float32
BF16 = jnp.bfloat16
LANES = 128
TOP = 8
FIXED = 6


def own_half():
    place = lax.axis_index("gy")
    half = (place & 1) ^ (lax.axis_index("gx") & 1)
    for bit in range(1, (lax.axis_size("gy") - 1).bit_length()):
        half = half ^ ((place >> bit) & 1)
    return half


def dft_tables(side):
    half = side // 2
    fold = LANES // half
    outer = side // fold
    per_row = LANES // side
    y_hi, parity, x = np.meshgrid(np.arange(fold), np.arange(per_row), np.arange(side), indexing="ij")
    y_hi, parity, x = y_hi.reshape(-1, 1), parity.reshape(-1, 1), x.reshape(-1, 1)
    out_par, part, u_lo, v = np.meshgrid(
        np.arange(per_row), np.arange(2), np.arange(fold), np.arange(half), indexing="ij"
    )
    out_par, part, u_lo, v = (t.reshape(1, -1) for t in (out_par, part, u_lo, v))
    turns = (v * x + outer * u_lo * y_hi) % side
    angle = 2.0 * np.pi * turns / side
    table = np.where(part == 0, np.cos(angle), -np.sin(angle)) / side
    table = np.where(parity == out_par, table, 0.0).astype(np.float32)
    high = table.astype(BF16)
    low = (table - high.astype(np.float32)).astype(BF16)
    lane_u = np.arange(LANES) // half
    turn = (np.arange(outer)[:, None] * lane_u[None, :]) % side
    angle = 2.0 * np.pi * turn / side
    twiddle = np.stack([np.cos(angle), np.sin(angle)], 1).astype(np.float32)
    turn = 2.0 * np.pi * np.arange(side) / side
    wave = np.concatenate([np.cos(turn), np.sin(turn)]).astype(np.float32)
    return high, low, twiddle.reshape(2 * outer, LANES), np.tile(wave[None], (8, 1))


def butterflies(real, imag):
    count = len(real)
    if count == 1:
        return real, imag
    even_r, even_i = butterflies(real[0::2], imag[0::2])
    odd_r, odd_i = butterflies(real[1::2], imag[1::2])
    top_r, top_i, low_r, low_i = [], [], [], []
    for k in range(count // 2):
        c = math.cos(2.0 * math.pi * k / count)
        s = math.sin(2.0 * math.pi * k / count)
        r, i = odd_r[k], odd_i[k]
        if k == 0:
            tr, ti = r, i
        elif 4 * k == count:
            tr, ti = i, -r
        elif 8 * k == count:
            tr, ti = (r + i) * c, (i - r) * c
        elif 8 * k == 3 * count:
            tr, ti = (i - r) * s, -(r + i) * s
        else:
            tr, ti = r * c + i * s, i * c - r * s
        top_r.append(even_r[k] + tr)
        top_i.append(even_i[k] + ti)
        low_r.append(even_r[k] - tr)
        low_i.append(even_i[k] - ti)
    return top_r + low_r, top_i + low_i


def split(value):
    high = value.astype(BF16)
    return high, (value - high.astype(F32)).astype(BF16)


def spectra_body(
    ids_far, images_far, high_far, low_far, twiddle_far, wave_far, offsets_far, ctf_far, noise_far, slots_far, priors_far,
    rotated, squares, powers, data_power, prior,
    ids, images, high, low, twiddle, wave, offsets, ctf, noise, slots, priors,
    stacked, partial, rows, w_real, w_imag, cosine, sine, inverse, total, arrived,
):
    copies = [
        pltpu.make_async_copy(far, near, arrived.at[j])
        for j, (far, near) in enumerate((
            (offsets_far, offsets), (wave_far, wave), (noise_far, noise), (slots_far, slots), (priors_far, priors),
            (images_far, images), (high_far, high), (low_far, low), (ids_far, ids), (ctf_far, ctf), (twiddle_far, twiddle),
        ))
    ]
    for copy in copies:
        copy.start()
    count, pixels = images.shape
    side = math.isqrt(pixels)
    half = side // 2
    fold = LANES // half
    outer = side // fold
    per_row = LANES // side
    groups = outer // per_row
    shifts = offsets.shape[1]
    columns = noise.shape[1] // LANES
    width = noise.shape[1]

    for copy in copies[:5]:
        copy.wait()
    inverse[...] = 1.0 / noise[...]
    lane = lax.broadcasted_iota(jnp.int32, (shifts, LANES), 1)
    shift = lax.broadcasted_iota(jnp.int32, (shifts, LANES), 0)
    step_u = jnp.zeros((shifts, LANES), jnp.int32)
    step_v = jnp.zeros((shifts, LANES), jnp.int32)
    for s in range(shifts):
        step_u = jnp.where(shift == s, offsets[0, s], step_u)
        step_v = jnp.where(shift == s, offsets[1, s], step_v)
    for column in range(columns):
        u = lane // half + fold * column
        turn = (u * step_u + (lane % half) * step_v) & (side - 1)
        at = slice(column * LANES, (column + 1) * LANES)
        cosine[:, at] = jnp.take_along_axis(wave[...], turn, axis=1)
        sine[:, at] = jnp.take_along_axis(wave[...], turn + side, axis=1)

    classes = slots.shape[0]
    scored = prior.shape[0]
    rest = scored // classes - TOP
    line = lax.broadcasted_iota(jnp.int32, prior.shape, 0)
    owner = jnp.where(line < classes * TOP, line // TOP, (line - classes * TOP) // rest)
    ring = lax.axis_index("gx")
    value = jnp.zeros(prior.shape, F32)
    for d in range(classes):
        value = jnp.where(owner == d, priors[slots[lax.rem(ring - d + classes, classes)]], value)
    prior[...] = value

    for copy in copies[5:8]:
        copy.wait()
    for m in range(groups):
        for y in range(fold):
            source = (m + groups * y) * LANES
            stacked[m * count:(m + 1) * count, y * LANES:(y + 1) * LANES] = images[:, source:source + LANES]
    partial[...] = jnp.dot(stacked[...], high[...], preferred_element_type=F32)
    partial[...] += jnp.dot(stacked[...], low[...], preferred_element_type=F32)

    for copy in copies[8:]:
        copy.wait()

    def fetch(p, carry):
        rows[pl.ds(p, 1), :] = ctf[pl.ds(ids[p], 1), :]
        return carry

    lax.fori_loop(0, count, fetch, 0, unroll=16)

    def transform(block, carry):
        base = block * 8
        real, imag = [], []
        for y in range(outer):
            m, parity = y // per_row, y % per_row
            row = pl.ds(m * count + base, 8)
            r = partial[row, (2 * parity) * LANES:(2 * parity + 1) * LANES]
            i = partial[row, (2 * parity + 1) * LANES:(2 * parity + 2) * LANES]
            if y:
                c = twiddle[2 * y:2 * y + 1, :]
                s = twiddle[2 * y + 1:2 * y + 2, :]
                r, i = r * c + i * s, i * c - r * s
            real.append(r)
            imag.append(i)
        real, imag = butterflies(real, imag)
        here = pl.ds(base, 8)
        energy = jnp.zeros((8, LANES), F32)
        for column in range(columns):
            at = slice(column * LANES, (column + 1) * LANES)
            inv = inverse[:, at]
            whiten = rows[here, at] * inv
            r, i = real[column], imag[column]
            energy += (r * r + i * i) * inv
            w_real[here, at] = (r * whiten).astype(BF16).astype(F32)
            w_imag[here, at] = (i * whiten).astype(BF16).astype(F32)
        total[here, :] = energy
        return carry

    lax.fori_loop(0, count // 8, transform, 0)
    energy = jnp.sum(jnp.transpose(total[...]), axis=0, keepdims=True)
    data_power[...] = jnp.concatenate([energy] * (data_power.shape[1] // count), axis=1)

    def rotate(column, carry):
        at = pl.ds(pl.multiple_of(column * LANES, LANES), LANES)
        square = rows[:, at] * rows[:, at]
        high, low = split(square)
        squares[column, 0:count, :] = high
        squares[column, count:, :] = low
        high, low = split(square * inverse[:, at])
        powers[column, 0:count, :] = high
        powers[column, count:, :] = low
        wr, wi = w_real[:, at], w_imag[:, at]
        for s in range(shifts):
            c, n = cosine[s:s + 1, at], sine[s:s + 1, at]
            rotated[column, s * count:(s + 1) * count, :] = (wr * c - wi * n).astype(BF16)
            rotated[columns + column, s * count:(s + 1) * count, :] = (wi * c + wr * n).astype(BF16)
        return carry

    lax.fori_loop(0, columns, rotate, 0)


def spectra(group_ids, particles, shift_offsets, ctf_table, noise_power, slot_class, log_prior, rotations):
    count, pixels = particles.shape
    side = math.isqrt(pixels)
    width = noise_power.shape[0]
    shifts = shift_offsets.shape[0]
    high, low, twiddle, wave = dft_tables(side)
    vmem = pl.BlockSpec(memory_space=pltpu.VMEM)
    far = pl.BlockSpec(memory_space=pltpu.HBM)
    shape = pltpu.VMEM
    columns = width // LANES
    plane = shape((columns, 2 * count, LANES), BF16)
    scored = shape((slot_class.shape[0] * rotations, LANES), F32)
    k = high.shape[0]
    groups = pixels // k
    return pl.pallas_call(
        spectra_body,
        out_shape=(shape((2 * columns, shifts * count, LANES), BF16), plane, plane, shape((1, 2 * count), F32), scored),
        cost_estimate=pl.CostEstimate(flops=2**32, transcendentals=0, bytes_accessed=2**23),
        in_specs=[far] * 11,
        out_specs=(vmem,) * 5,
        scratch_shapes=[
            pltpu.SMEM(group_ids.shape, jnp.int32),
            pltpu.VMEM(particles.shape, particles.dtype),
            pltpu.VMEM(high.shape, BF16),
            pltpu.VMEM(low.shape, BF16),
            pltpu.VMEM(twiddle.shape, F32),
            pltpu.VMEM(wave.shape, F32),
            pltpu.SMEM(shift_offsets.shape[::-1], jnp.int32),
            pltpu.VMEM(ctf_table.shape, F32),
            pltpu.VMEM((1, width), F32),
            pltpu.SMEM(slot_class.shape, jnp.int32),
            pltpu.SMEM(log_prior.shape, F32),
            pltpu.VMEM((groups * count, k), BF16),
            pltpu.VMEM((groups * count, high.shape[1]), F32),
            pltpu.VMEM((count, width), F32),
            pltpu.VMEM((count, width), F32),
            pltpu.VMEM((count, width), F32),
            pltpu.VMEM((shifts, width), F32),
            pltpu.VMEM((shifts, width), F32),
            pltpu.VMEM((1, width), F32),
            pltpu.VMEM((count, LANES), F32),
            pltpu.SemaphoreType.DMA((11,)),
        ],
        compiler_params=pltpu.CompilerParams(vmem_limit_bytes=24 * 2**20),
        name="spectra",
    )(*(
        pltpu.with_memory_space_constraint(x, pltpu.HBM)
        for x in (
            group_ids, particles, jnp.asarray(high), jnp.asarray(low), jnp.asarray(twiddle), jnp.asarray(wave),
            shift_offsets.T, ctf_table, noise_power.reshape(1, width), slot_class, log_prior,
        )
    ))


def dot_rows(a, b):
    return lax.dot_general(a, b, (((1,), (1,)), ((), ())), preferred_element_type=F32)


def side_by_side(planes, first, count):
    return jnp.concatenate([planes[first + j] for j in range(count)], axis=1)


def fold(value):
    rest = value.shape[0] - TOP
    pieces = TOP // rest
    step = value.shape[1] // pieces
    tail = jnp.concatenate([value[TOP:, j * step:(j + 1) * step] for j in range(pieces)], axis=0)
    return jnp.concatenate([value[:TOP], tail], axis=1)


def folded_width(rotations, width):
    return width + (rotations - TOP) * width // TOP


def pack_body(far, mine, theirs, near, arrived):
    width = near.shape[2]
    h = own_half()
    copies = []
    for j, half in enumerate((h, 1 - h)):
        source = far.at[0, :, pl.ds(pl.multiple_of(half * width, width), width)]
        copies.append(pltpu.make_async_copy(source, near.at[j], arrived.at[j]))
    for copy in copies:
        copy.start()
    for j, out in enumerate((mine, theirs)):
        copies[j].wait()
        out[...] = fold(near[j].astype(F32)).astype(BF16)


def pack(references):
    _, rotations, full = references.shape
    width = full // 2
    vmem = pl.BlockSpec(memory_space=pltpu.VMEM)
    out = pltpu.VMEM((TOP, folded_width(rotations, width)), BF16)
    return pl.pallas_call(
        pack_body,
        out_shape=(out, out),
        in_specs=[pl.BlockSpec(memory_space=pltpu.HBM)],
        out_specs=(vmem, vmem),
        scratch_shapes=[pltpu.VMEM((2, rotations, width), BF16), pltpu.SemaphoreType.DMA((2,))],
        compiler_params=pltpu.CompilerParams(vmem_limit_bytes=4 * 2**20),
        name="pack",
    )(pltpu.with_memory_space_constraint(references, pltpu.HBM))


def half_scores(h, rotated, powers, packed, stack):
    classes = len(packed)
    rows, width = stack.shape
    rest = rows // classes - TOP
    pieces = TOP // rest
    step = width // pieces
    for d, ref in enumerate(packed):
        value = ref[...].astype(F32)
        stack[d * TOP:(d + 1) * TOP, :] = value[:, :width]
        low = classes * TOP + d * rest
        for j in range(pieces):
            stack[low:low + rest, j * step:(j + 1) * step] = value[j * rest:(j + 1) * rest, width:]
    planes = width // LANES
    value = stack[...]
    inter = dot_rows(value.astype(BF16), side_by_side(rotated, h * planes, planes))
    high, low = split(value * value)
    power = dot_rows(jnp.concatenate([high, low], axis=0), side_by_side(powers, 0, planes))
    power = power[:rows] + power[rows:]
    power = 0.5 * (power + pltpu.roll(power, power.shape[1] // 2, axis=1))
    return [inter[:, j:j + LANES] - power for j in range(0, inter.shape[1], LANES)]


def first_body(rotated, powers, *refs):
    *packed, scores, stack = refs
    parts = half_scores(own_half(), rotated, powers, packed, stack)
    for j, part in enumerate(parts):
        scores[:, j * LANES:(j + 1) * LANES] = part


def half_sums(half, soft, by_class, digits, rotated, squares, out):
    classes = out.shape[0]
    rows = soft.shape[0]
    rest = rows // classes - TOP
    planes = rotated.shape[0] // 2
    width = planes * LANES
    pieces = TOP // rest
    step = width // pieces
    sums = jnp.dot(soft, side_by_side(rotated, half * planes, planes), preferred_element_type=F32)
    narrow = planes // 2
    extra = jnp.dot(by_class, side_by_side(squares, half * narrow, narrow), preferred_element_type=F32)
    extra = extra[:classes] + extra[extra.shape[0] // 2:extra.shape[0] // 2 + classes]
    at = width + step
    for d in range(classes):
        out[d, :, 0:width] = sums[d * TOP:(d + 1) * TOP, :].astype(out.dtype)
        low = sums[classes * TOP + d * rest:classes * TOP + (d + 1) * rest, :]
        tail = jnp.concatenate([low[:, j * step:(j + 1) * step] for j in range(pieces)], axis=0)
        out[d, :, width:at] = tail.astype(out.dtype)
        lines = extra[d:d + 1, :]
        tall = jnp.concatenate([lines[:, j * LANES:(j + 1) * LANES] for j in range(narrow)], axis=0)
        out[d, :, at:at + LANES] = tall.astype(out.dtype)
        out[d, :, at + LANES:at + 2 * LANES] = digits.astype(out.dtype)


def second_body(digit_bits, rotated, powers, squares, data_power, prior, scores, *refs):
    *packed, send, soft_out, class_out, digits_out, stack = refs
    classes = len(packed)
    rows = scores.shape[0]
    rest = rows // classes - TOP
    count = powers.shape[1] // 2
    there = 1 - own_half()
    parts = half_scores(there, rotated, powers, packed, stack)
    energy = 0.5 * data_power[...]
    logits = [
        ((scores[:, j * LANES:(j + 1) * LANES] + part) - energy) + prior[...] for j, part in enumerate(parts)
    ]
    top = jnp.max(functools.reduce(jnp.maximum, logits), axis=0, keepdims=True)
    top = jnp.maximum(top, pltpu.roll(top, count, axis=1))
    raised = [jnp.exp(l - top) for l in logits]
    norm = jnp.sum(functools.reduce(jnp.add, raised), axis=0, keepdims=True)
    norm = norm + pltpu.roll(norm, count, axis=1)
    scale = 1.0 / norm
    weights = [r * scale for r in raised]
    soft = jnp.concatenate([w.astype(BF16) for w in weights], axis=1)
    soft_out[...] = soft

    weight = functools.reduce(jnp.add, weights)
    weight = weight + pltpu.roll(weight, count, axis=1)
    base = classes * TOP
    per_class = jnp.concatenate(
        [
            jnp.sum(weight[d * TOP:(d + 1) * TOP], axis=0, keepdims=True)
            + jnp.sum(weight[base + d * rest:base + (d + 1) * rest], axis=0, keepdims=True)
            for d in range(classes)
        ]
        + [jnp.zeros((-classes % 8, LANES), F32)] * (1 if classes % 8 else 0),
        axis=0,
    )
    high = per_class.astype(BF16).astype(F32)
    lane = lax.broadcasted_iota(jnp.int32, per_class.shape, 1)
    by_class = jnp.concatenate([high, jnp.where(lane < count, per_class - high, 0.0)], axis=0).astype(BF16)
    class_out[...] = by_class

    lane = lax.broadcasted_iota(jnp.int32, (1, LANES), 1)
    evidence = jnp.sum(jnp.where(lane < count, top + jnp.log(norm), 0.0), axis=1, keepdims=True)
    number = jnp.round(jnp.broadcast_to(evidence, (1, LANES)) * float(2**FIXED)).astype(jnp.int32)
    digit = lax.shift_right_logical(jnp.abs(number), jnp.minimum(lane * digit_bits, 31))
    digit = jnp.where(lane * digit_bits < 31, digit & (2**digit_bits - 1), 0)
    digit = jnp.where(number < 0, -digit, digit).astype(F32)
    digits = jnp.broadcast_to(digit, (TOP, LANES))
    digits_out[...] = digits
    half_sums(there, soft, by_class, digits, rotated, squares, send)


def third_body(rotated, squares, soft, by_class, digits, keep):
    half_sums(own_half(), soft[...], by_class[...], digits[...], rotated, squares, keep)


def local_call(body, out_shape, operands, scratch, name):
    chip = pl.BlockSpec(memory_space=pltpu.VMEM)
    return pl.pallas_call(
        body,
        out_shape=out_shape,
        in_specs=[chip] * len(operands),
        out_specs=jax.tree.map(lambda _: chip, out_shape, is_leaf=lambda x: not isinstance(x, tuple)),
        scratch_shapes=scratch,
        compiler_params=pltpu.CompilerParams(vmem_limit_bytes=16 * 2**20),
        cost_estimate=pl.CostEstimate(flops=2**31, transcendentals=0, bytes_accessed=2**21),
        name=name,
    )(*(pltpu.with_memory_space_constraint(x, pltpu.VMEM) for x in operands))


def finish_body(owned, other, scale, sums, ctf_power, log_evidence):
    rotations, _, full = sums.shape
    width = full // 2
    rest = rotations - TOP
    pieces = TOP // rest
    step = width // pieces
    at = width + step
    narrow = width // 2
    h = own_half()
    for half, source in ((h, owned), (1 - h, other)):
        sums[0:TOP, 0, pl.ds(pl.multiple_of(half * width, width), width)] = source[:, :width]
        for j in range(pieces):
            here = pl.ds(pl.multiple_of(half * width + j * step, step), step)
            sums[TOP:, 0, here] = source[j * rest:(j + 1) * rest, width:at]
        for j in range(narrow // LANES):
            here = pl.ds(pl.multiple_of(half * narrow + j * LANES, LANES), LANES)
            ctf_power[:, here] = source[j:j + 1, at:at + LANES]
    log_evidence[...] = jnp.sum(owned[0:1, at + LANES:at + 2 * LANES] * scale[...], axis=1, keepdims=True)


def finish(owned, other, rotations, width, scale):
    vmem = pl.BlockSpec(memory_space=pltpu.VMEM)
    shape = jax.ShapeDtypeStruct
    return pl.pallas_call(
        finish_body,
        out_shape=(shape((rotations, 1, 2 * width), F32), shape((1, width), F32), shape((1, 1), F32)),
        in_specs=[vmem] * 3,
        out_specs=(vmem,) * 3,
        compiler_params=pltpu.CompilerParams(vmem_limit_bytes=8 * 2**20),
        name="finish",
    )(owned, other, scale)


def tree(parts):
    while len(parts) > 1:
        middle = len(parts) // 2
        parts = [parts[j] + parts[j + middle] for j in range(middle)]
    return parts[0]


def pairwise(parts):
    while len(parts) > 1:
        parts = [a + b for a, b in zip(parts[0::2], parts[1::2], strict=True)]
    return parts[0]


def shards(
    particles, references, slot_class, log_prior, shift_offsets, group_ids, ctf_table, noise_power
):
    rings = lax.axis_size("gx")
    spread = lax.axis_size("gy")
    chips = spread // 2
    count = particles.shape[0]
    width = noise_power.shape[0]
    rotations = references.shape[1]
    digit_bits = max(1, 8 - (rings * spread - 1).bit_length())

    def move(value, rule):
        pairs = []
        for z in range(rings):
            for c in range(chips):
                for core in range(2):
                    z2, c2, core2 = rule(z, c, core)
                    pairs.append((z * spread + 2 * c + core, z2 * spread + 2 * c2 + core2))
        return lax.ppermute(value, ("gx", "gy"), pairs)

    def shift(d):
        return lambda z, c, core: ((z + d) % rings, c, core ^ (d & 1))

    def swap(z, c, core):
        return z, c, core ^ 1

    def hop(mask):
        return lambda z, c, core: (z, c ^ mask, core ^ (bin(mask).count("1") & 1))

    near, far = pack(references)
    mine = [move(near, shift(d)) for d in range(1, rings)]
    spectra_out = spectra(
        group_ids, particles, shift_offsets, ctf_table, noise_power, slot_class, log_prior, rotations
    )
    mine, near, far, spectra_out = lax.optimization_barrier((mine, near, far, spectra_out))
    rotated, squares, powers, data_power, prior = spectra_out
    theirs = [move(value, swap) for value in mine]
    rows = rings * rotations
    planes = rotated.shape[1]
    stack = pltpu.VMEM((rows, width), F32)
    scores = local_call(first_body, pltpu.VMEM((rows, planes), F32), (rotated, powers, near, *mine), [stack], "first")
    theirs, scores = lax.optimization_barrier((theirs, scores))
    block = (rings, TOP, folded_width(rotations, width) + 2 * LANES)
    send, soft, by_class, digits = local_call(
        functools.partial(second_body, digit_bits),
        (
            pltpu.VMEM(block, BF16),
            pltpu.VMEM((rows, planes), BF16),
            pltpu.VMEM((2 * (rings + -rings % 8), LANES), BF16),
            pltpu.VMEM((TOP, LANES), F32),
        ),
        (rotated, powers, squares, data_power, prior, scores, far, *theirs),
        [stack],
        "second",
    )
    arrived = move(send, swap)
    keep = local_call(
        third_body, pltpu.VMEM(block, F32), (rotated, squares, soft, by_class, digits), [], "third"
    )
    arrived, keep = lax.optimization_barrier((arrived, keep))
    pair = keep + arrived.astype(F32)
    gathered = [pair[0]]
    for d in range(1, rings):
        gathered.append(move(pair[d].astype(BF16), shift(rings - d)).astype(F32))
    owned = tree(gathered)
    low = owned.astype(BF16)
    parts = [low] + [move(low, hop(mask)) for mask in range(1, chips)]
    owned = pairwise([part.astype(F32) for part in parts])
    other = move(owned, swap)
    scale = np.zeros((1, LANES), np.float64)
    for j in range(-(-31 // digit_bits)):
        scale[0, j] = 2.0 ** (j * digit_bits - FIXED)
    scale = scale / (count * rings * spread * width)
    sums, ctf_power, log_evidence = finish(owned, other, rotations, width, jnp.asarray(scale, F32))
    return sums.reshape(1, rotations, 2 * width), ctf_power, log_evidence.reshape(())


def solution(mesh):
    return jax.shard_map(
        shards,
        mesh=mesh,
        in_specs=(
            P(("gx", "gy"), None),
            P("gx", None, None),
            P(),
            P(),
            P(),
            P(("gx", "gy")),
            P(),
            P(),
        ),
        out_specs=(P("gx", None, None), P("gx", None), P()),
        check_vma=False,
    )
```

```python
import functools
import math

import jax
import jax.numpy as jnp
import numpy as np
from jax import lax
from jax.experimental import pallas as pl
from jax.experimental.pallas import tpu as pltpu
from jax.sharding import PartitionSpec as P

F32 = jnp.float32
BF16 = jnp.bfloat16
LANES = 128
TOP = 8
FIXED = 6


def own_half():
    place = lax.axis_index("gy")
    half = (place & 1) ^ (lax.axis_index("gx") & 1)
    for bit in range(1, (lax.axis_size("gy") - 1).bit_length()):
        half = half ^ ((place >> bit) & 1)
    return half


def dft_tables(side):
    half = side // 2
    fold = LANES // half
    outer = side // fold
    per_row = LANES // side
    y_hi, parity, x = np.meshgrid(np.arange(fold), np.arange(per_row), np.arange(side), indexing="ij")
    y_hi, parity, x = y_hi.reshape(-1, 1), parity.reshape(-1, 1), x.reshape(-1, 1)
    out_par, part, u_lo, v = np.meshgrid(
        np.arange(per_row), np.arange(2), np.arange(fold), np.arange(half), indexing="ij"
    )
    out_par, part, u_lo, v = (t.reshape(1, -1) for t in (out_par, part, u_lo, v))
    turns = (v * x + outer * u_lo * y_hi) % side
    angle = 2.0 * np.pi * turns / side
    table = np.where(part == 0, np.cos(angle), -np.sin(angle)) / side
    table = np.where(parity == out_par, table, 0.0).astype(np.float32)
    high = table.astype(BF16)
    low = (table - high.astype(np.float32)).astype(BF16)
    pair = np.concatenate([high, low], axis=0)
    lane_u = np.arange(LANES) // half
    turn = (np.arange(outer)[:, None] * lane_u[None, :]) % side
    angle = 2.0 * np.pi * turn / side
    twiddle = np.stack([np.cos(angle), np.sin(angle)], 1).astype(np.float32)
    turn = 2.0 * np.pi * np.arange(side) / side
    wave = np.concatenate([np.cos(turn), np.sin(turn)]).astype(np.float32)
    return pair, twiddle.reshape(2 * outer, LANES), np.tile(wave[None], (8, 1))


def butterflies(real, imag):
    count = len(real)
    if count == 1:
        return real, imag
    even_r, even_i = butterflies(real[0::2], imag[0::2])
    odd_r, odd_i = butterflies(real[1::2], imag[1::2])
    top_r, top_i, low_r, low_i = [], [], [], []
    for k in range(count // 2):
        c = math.cos(2.0 * math.pi * k / count)
        s = math.sin(2.0 * math.pi * k / count)
        r, i = odd_r[k], odd_i[k]
        if k == 0:
            tr, ti = r, i
        elif 4 * k == count:
            tr, ti = i, -r
        elif 8 * k == count:
            tr, ti = (r + i) * c, (i - r) * c
        elif 8 * k == 3 * count:
            tr, ti = (i - r) * s, -(r + i) * s
        else:
            tr, ti = r * c + i * s, i * c - r * s
        top_r.append(even_r[k] + tr)
        top_i.append(even_i[k] + ti)
        low_r.append(even_r[k] - tr)
        low_i.append(even_i[k] - ti)
    return top_r + low_r, top_i + low_i


def split(value):
    high = value.astype(BF16)
    return high, (value - high.astype(F32)).astype(BF16)


def spectra_body(
    ids_near, offsets_near, slots_near, priors_near, images, pair, twiddle, wave, ctf, noise,
    rotated, squares, powers, data_power, prior,
    ids, partial, rows, w_real, w_imag, cosine, sine, inverse, total, arrived,
):
    copy = pltpu.make_async_copy(ids_near, ids, arrived.at[0])
    copy.start()
    count, pixels = images.shape
    side = math.isqrt(pixels)
    half = side // 2
    fold = LANES // half
    outer = side // fold
    per_row = LANES // side
    groups = outer // per_row
    shifts = cosine.shape[0]
    columns = noise.shape[1] // LANES

    tall = []
    for m in range(groups):
        tall.append(jnp.concatenate(
            [images[:, (m + groups * y) * LANES:(m + groups * y + 1) * LANES] for y in range(fold)], axis=1
        ))
    tall = jnp.concatenate(tall, axis=0)
    partial[...] = jnp.dot(jnp.concatenate([tall, tall], axis=1), pair[...], preferred_element_type=F32)
    inverse[...] = 1.0 / noise[...]
    lane = lax.broadcasted_iota(jnp.int32, (shifts, LANES), 1)
    shift = lax.broadcasted_iota(jnp.int32, (shifts, LANES), 0)
    step_u = jnp.zeros((shifts, LANES), jnp.int32)
    step_v = jnp.zeros((shifts, LANES), jnp.int32)
    for s in range(shifts):
        step_u = jnp.where(shift == s, offsets_near[0:1, s:s + 1], step_u)
        step_v = jnp.where(shift == s, offsets_near[1:2, s:s + 1], step_v)
    for column in range(columns):
        u = lane // half + fold * column
        turn = (u * step_u + (lane % half) * step_v) & (side - 1)
        at = slice(column * LANES, (column + 1) * LANES)
        cosine[:, at] = jnp.take_along_axis(wave[...], turn, axis=1)
        sine[:, at] = jnp.take_along_axis(wave[...], turn + side, axis=1)

    classes = slots_near.shape[1]
    scored = prior.shape[0]
    rest = scored // classes - TOP
    line = lax.broadcasted_iota(jnp.int32, prior.shape, 0)
    owner = jnp.where(line < classes * TOP, line // TOP, (line - classes * TOP) // rest)
    slot = lax.rem(lax.axis_index("gx") - owner + classes, classes)
    value = jnp.zeros(prior.shape, F32)
    by_slot = jnp.zeros((1, classes), F32)
    for d in range(classes):
        by_slot = jnp.where(slots_near[...] == d, priors_near[:, d:d + 1], by_slot)
    for d in range(classes):
        value = jnp.where(slot == d, by_slot[:, d:d + 1], value)
    prior[...] = value
    copy.wait()

    def transform(block, carry):
        base = block * 8
        for p in range(8):
            rows[pl.ds(base + p, 1), :] = ctf[pl.ds(ids[base + p], 1), :]
        real, imag = [], []
        for y in range(outer):
            m, parity = y // per_row, y % per_row
            row = pl.ds(m * count + base, 8)
            r = partial[row, (2 * parity) * LANES:(2 * parity + 1) * LANES]
            i = partial[row, (2 * parity + 1) * LANES:(2 * parity + 2) * LANES]
            if y:
                c = twiddle[2 * y:2 * y + 1, :]
                s = twiddle[2 * y + 1:2 * y + 2, :]
                r, i = r * c + i * s, i * c - r * s
            real.append(r)
            imag.append(i)
        real, imag = butterflies(real, imag)
        here = pl.ds(base, 8)
        energy = jnp.zeros((8, LANES), F32)
        for column in range(columns):
            at = slice(column * LANES, (column + 1) * LANES)
            inv = inverse[:, at]
            whiten = rows[here, at] * inv
            r, i = real[column], imag[column]
            energy += (r * r + i * i) * inv
            w_real[here, at] = (r * whiten).astype(BF16).astype(F32)
            w_imag[here, at] = (i * whiten).astype(BF16).astype(F32)
        total[here, :] = energy
        return carry

    lax.fori_loop(0, count // 8, transform, 0)
    energy = jnp.sum(jnp.transpose(total[...]), axis=0, keepdims=True)
    data_power[...] = jnp.concatenate([energy] * (data_power.shape[1] // count), axis=1)

    def rotate(column, carry):
        at = pl.ds(pl.multiple_of(column * LANES, LANES), LANES)
        square = rows[:, at] * rows[:, at]
        high, low = split(square)
        squares[column, 0:count, :] = high
        squares[column, count:, :] = low
        high, low = split(square * inverse[:, at])
        powers[column, 0:count, :] = high
        powers[column, count:, :] = low
        wr, wi = w_real[:, at], w_imag[:, at]
        for s in range(shifts):
            c, n = cosine[s:s + 1, at], sine[s:s + 1, at]
            rotated[column, s * count:(s + 1) * count, :] = (wr * c - wi * n).astype(BF16)
            rotated[columns + column, s * count:(s + 1) * count, :] = (wi * c + wr * n).astype(BF16)
        return carry

    lax.fori_loop(0, columns, rotate, 0)


def spectra(group_ids, particles, shift_offsets, ctf_table, noise_power, slot_class, log_prior, rotations):
    count, pixels = particles.shape
    side = math.isqrt(pixels)
    width = noise_power.shape[0]
    shifts = shift_offsets.shape[0]
    pair, twiddle, wave = dft_tables(side)
    vmem = pl.BlockSpec(memory_space=pltpu.VMEM)
    shape = pltpu.VMEM
    columns = width // LANES
    plane = shape((columns, 2 * count, LANES), BF16)
    scored = shape((slot_class.shape[0] * rotations, LANES), F32)
    k = pair.shape[0] // 2
    groups = pixels // k
    return pl.pallas_call(
        spectra_body,
        out_shape=(shape((2 * columns, shifts * count, LANES), BF16), plane, plane, shape((1, 2 * count), F32), scored),
        cost_estimate=pl.CostEstimate(flops=2**32, transcendentals=0, bytes_accessed=2**23),
        in_specs=[vmem] * 10,
        out_specs=(vmem,) * 5,
        scratch_shapes=[
            pltpu.SMEM(group_ids.shape, jnp.int32),
            pltpu.VMEM((groups * count, pair.shape[1]), F32),
            pltpu.VMEM((count, width), F32),
            pltpu.VMEM((count, width), F32),
            pltpu.VMEM((count, width), F32),
            pltpu.VMEM((shifts, width), F32),
            pltpu.VMEM((shifts, width), F32),
            pltpu.VMEM((1, width), F32),
            pltpu.VMEM((count, LANES), F32),
            pltpu.SemaphoreType.DMA((1,)),
        ],
        compiler_params=pltpu.CompilerParams(vmem_limit_bytes=24 * 2**20),
        name="spectra",
    )(*(
        pltpu.with_memory_space_constraint(x, pltpu.VMEM)
        for x in (
            group_ids, shift_offsets.T, slot_class.reshape(1, -1), log_prior.reshape(1, -1), particles, jnp.asarray(pair), jnp.asarray(twiddle),
            jnp.asarray(wave), ctf_table, noise_power.reshape(1, width),
        )
    ))


def dot_rows(a, b):
    return lax.dot_general(a, b, (((1,), (1,)), ((), ())), preferred_element_type=F32)


def side_by_side(planes, first, count):
    return jnp.concatenate([planes[first + j] for j in range(count)], axis=1)


def fold(value):
    rest = value.shape[0] - TOP
    pieces = TOP // rest
    step = value.shape[1] // pieces
    tail = jnp.concatenate([value[TOP:, j * step:(j + 1) * step] for j in range(pieces)], axis=0)
    return jnp.concatenate([value[:TOP], tail], axis=1)


def folded_width(rotations, width):
    return width + (rotations - TOP) * width // TOP


def pack_body(far, mine, theirs, near, arrived):
    width = near.shape[2]
    h = own_half()
    copies = []
    for j, half in enumerate((h, 1 - h)):
        source = far.at[0, :, pl.ds(pl.multiple_of(half * width, width), width)]
        copies.append(pltpu.make_async_copy(source, near.at[j], arrived.at[j]))
    for copy in copies:
        copy.start()
    for j, out in enumerate((mine, theirs)):
        copies[j].wait()
        out[...] = fold(near[j].astype(F32)).astype(BF16)


def pack(references):
    _, rotations, full = references.shape
    width = full // 2
    vmem = pl.BlockSpec(memory_space=pltpu.VMEM)
    out = pltpu.VMEM((TOP, folded_width(rotations, width)), BF16)
    return pl.pallas_call(
        pack_body,
        out_shape=(out, out),
        in_specs=[pl.BlockSpec(memory_space=pltpu.HBM)],
        out_specs=(vmem, vmem),
        scratch_shapes=[pltpu.VMEM((2, rotations, width), BF16), pltpu.SemaphoreType.DMA((2,))],
        cost_estimate=pl.CostEstimate(flops=2**33, transcendentals=0, bytes_accessed=2**20),
        compiler_params=pltpu.CompilerParams(vmem_limit_bytes=4 * 2**20),
        name="pack",
    )(pltpu.with_memory_space_constraint(references, pltpu.HBM))


def half_scores(h, rotated, powers, packed, stack):
    classes = len(packed)
    rows, width = stack.shape
    rest = rows // classes - TOP
    pieces = TOP // rest
    step = width // pieces
    for d, ref in enumerate(packed):
        value = ref[...].astype(F32)
        stack[d * TOP:(d + 1) * TOP, :] = value[:, :width]
        low = classes * TOP + d * rest
        for j in range(pieces):
            stack[low:low + rest, j * step:(j + 1) * step] = value[j * rest:(j + 1) * rest, width:]
    planes = width // LANES
    value = stack[...]
    inter = dot_rows(value.astype(BF16), side_by_side(rotated, h * planes, planes))
    high, low = split(value * value)
    power = dot_rows(jnp.concatenate([high, low], axis=0), side_by_side(powers, 0, planes))
    power = power[:rows] + power[rows:]
    power = 0.5 * (power + pltpu.roll(power, power.shape[1] // 2, axis=1))
    return [inter[:, j:j + LANES] - power for j in range(0, inter.shape[1], LANES)]


def first_body(rotated, powers, *refs):
    *packed, scores, stack = refs
    parts = half_scores(own_half(), rotated, powers, packed, stack)
    for j, part in enumerate(parts):
        scores[:, j * LANES:(j + 1) * LANES] = part


def half_sums(half, soft, by_class, digits, rotated, squares, out):
    classes = out.shape[0]
    rows = soft.shape[0]
    rest = rows // classes - TOP
    planes = rotated.shape[0] // 2
    width = planes * LANES
    pieces = TOP // rest
    step = width // pieces
    sums = jnp.dot(soft, side_by_side(rotated, half * planes, planes), preferred_element_type=F32)
    narrow = planes // 2
    extra = jnp.dot(by_class, side_by_side(squares, half * narrow, narrow), preferred_element_type=F32)
    extra = extra[:classes] + extra[extra.shape[0] // 2:extra.shape[0] // 2 + classes]
    at = width + step
    for d in range(classes):
        out[d, :, 0:width] = sums[d * TOP:(d + 1) * TOP, :].astype(out.dtype)
        low = sums[classes * TOP + d * rest:classes * TOP + (d + 1) * rest, :]
        tail = jnp.concatenate([low[:, j * step:(j + 1) * step] for j in range(pieces)], axis=0)
        out[d, :, width:at] = tail.astype(out.dtype)
        lines = extra[d:d + 1, :]
        tall = jnp.concatenate([lines[:, j * LANES:(j + 1) * LANES] for j in range(narrow)], axis=0)
        out[d, :, at:at + LANES] = tall.astype(out.dtype)
        out[d, :, at + LANES:at + 2 * LANES] = digits.astype(out.dtype)


def second_body(digit_bits, rotated, powers, squares, data_power, prior, scores, *refs):
    *packed, send, soft_out, class_out, digits_out, stack = refs
    classes = len(packed)
    rows = scores.shape[0]
    rest = rows // classes - TOP
    count = powers.shape[1] // 2
    there = 1 - own_half()
    parts = half_scores(there, rotated, powers, packed, stack)
    energy = 0.5 * data_power[...]
    logits = [
        ((scores[:, j * LANES:(j + 1) * LANES] + part) - energy) + prior[...] for j, part in enumerate(parts)
    ]
    top = jnp.max(functools.reduce(jnp.maximum, logits), axis=0, keepdims=True)
    top = jnp.maximum(top, pltpu.roll(top, count, axis=1))
    raised = [jnp.exp(l - top) for l in logits]
    norm = jnp.sum(functools.reduce(jnp.add, raised), axis=0, keepdims=True)
    norm = norm + pltpu.roll(norm, count, axis=1)
    scale = 1.0 / norm
    weights = [r * scale for r in raised]
    soft = jnp.concatenate([w.astype(BF16) for w in weights], axis=1)
    soft_out[...] = soft

    weight = functools.reduce(jnp.add, weights)
    weight = weight + pltpu.roll(weight, count, axis=1)
    base = classes * TOP
    per_class = jnp.concatenate(
        [
            jnp.sum(weight[d * TOP:(d + 1) * TOP], axis=0, keepdims=True)
            + jnp.sum(weight[base + d * rest:base + (d + 1) * rest], axis=0, keepdims=True)
            for d in range(classes)
        ]
        + [jnp.zeros((-classes % 8, LANES), F32)] * (1 if classes % 8 else 0),
        axis=0,
    )
    high = per_class.astype(BF16).astype(F32)
    lane = lax.broadcasted_iota(jnp.int32, per_class.shape, 1)
    by_class = jnp.concatenate([high, jnp.where(lane < count, per_class - high, 0.0)], axis=0).astype(BF16)
    class_out[...] = by_class

    lane = lax.broadcasted_iota(jnp.int32, (1, LANES), 1)
    evidence = jnp.sum(jnp.where(lane < count, top + jnp.log(norm), 0.0), axis=1, keepdims=True)
    number = jnp.round(jnp.broadcast_to(evidence, (1, LANES)) * float(2**FIXED)).astype(jnp.int32)
    digit = lax.shift_right_logical(jnp.abs(number), jnp.minimum(lane * digit_bits, 31))
    digit = jnp.where(lane * digit_bits < 31, digit & (2**digit_bits - 1), 0)
    digit = jnp.where(number < 0, -digit, digit).astype(F32)
    digits = jnp.broadcast_to(digit, (TOP, LANES))
    digits_out[...] = digits
    half_sums(there, soft, by_class, digits, rotated, squares, send)


def third_body(rotated, squares, soft, by_class, digits, keep):
    half_sums(own_half(), soft[...], by_class[...], digits[...], rotated, squares, keep)


def local_call(body, out_shape, operands, scratch):
    chip = pl.BlockSpec(memory_space=pltpu.VMEM)
    return pl.pallas_call(
        body,
        out_shape=out_shape,
        in_specs=[chip] * len(operands),
        out_specs=jax.tree.map(lambda _: chip, out_shape, is_leaf=lambda x: not isinstance(x, tuple)),
        scratch_shapes=scratch,
        compiler_params=pltpu.CompilerParams(vmem_limit_bytes=16 * 2**20),
        cost_estimate=pl.CostEstimate(flops=2**31, transcendentals=0, bytes_accessed=2**21),
    )(*(pltpu.with_memory_space_constraint(x, pltpu.VMEM) for x in operands))


def finish_body(owned, other, scale, sums, ctf_power, log_evidence):
    rotations, _, full = sums.shape
    width = full // 2
    rest = rotations - TOP
    pieces = TOP // rest
    step = width // pieces
    at = width + step
    narrow = width // 2
    h = own_half()
    for half, source in ((h, owned), (1 - h, other)):
        sums[0:TOP, 0, pl.ds(pl.multiple_of(half * width, width), width)] = source[:, :width]
        for j in range(pieces):
            here = pl.ds(pl.multiple_of(half * width + j * step, step), step)
            sums[TOP:, 0, here] = source[j * rest:(j + 1) * rest, width:at]
        for j in range(narrow // LANES):
            here = pl.ds(pl.multiple_of(half * narrow + j * LANES, LANES), LANES)
            ctf_power[:, here] = source[j:j + 1, at:at + LANES]
    log_evidence[...] = jnp.sum(owned[0:1, at + LANES:at + 2 * LANES] * scale[...], axis=1, keepdims=True)


def finish(owned, other, rotations, width, scale):
    vmem = pl.BlockSpec(memory_space=pltpu.VMEM)
    shape = jax.ShapeDtypeStruct
    return pl.pallas_call(
        finish_body,
        out_shape=(shape((rotations, 1, 2 * width), F32), shape((1, width), F32), shape((1, 1), F32)),
        in_specs=[vmem] * 3,
        out_specs=(vmem,) * 3,
        compiler_params=pltpu.CompilerParams(vmem_limit_bytes=8 * 2**20),
        name="finish",
    )(owned, other, scale)


def tree(parts):
    while len(parts) > 1:
        middle = len(parts) // 2
        parts = [parts[j] + parts[j + middle] for j in range(middle)]
    return parts[0]


def pairwise(parts):
    while len(parts) > 1:
        parts = [a + b for a, b in zip(parts[0::2], parts[1::2], strict=True)]
    return parts[0]


def shards(
    particles, references, slot_class, log_prior, shift_offsets, group_ids, ctf_table, noise_power
):
    rings = lax.axis_size("gx")
    spread = lax.axis_size("gy")
    chips = spread // 2
    count = particles.shape[0]
    width = noise_power.shape[0]
    rotations = references.shape[1]
    digit_bits = max(1, 8 - (rings * spread - 1).bit_length())

    def move(value, rule):
        pairs = []
        for z in range(rings):
            for c in range(chips):
                for core in range(2):
                    z2, c2, core2 = rule(z, c, core)
                    pairs.append((z * spread + 2 * c + core, z2 * spread + 2 * c2 + core2))
        return lax.ppermute(value, ("gx", "gy"), pairs)

    def shift(d):
        return lambda z, c, core: ((z + d) % rings, c, core ^ (d & 1))

    def swap(z, c, core):
        return z, c, core ^ 1

    def hop(mask):
        return lambda z, c, core: (z, c ^ mask, core ^ (bin(mask).count("1") & 1))

    near, far = pack(references)
    mine = []
    for d in range(1, rings):
        mine.append(move(near, shift(d)))
    spectra_out = spectra(
        group_ids, particles, shift_offsets, ctf_table, noise_power, slot_class, log_prior, rotations
    )
    mine, near, far, spectra_out = lax.optimization_barrier((mine, near, far, spectra_out))
    rotated, squares, powers, data_power, prior = spectra_out
    theirs = [move(value, swap) for value in mine]
    rows = rings * rotations
    planes = rotated.shape[1]
    stack = pltpu.VMEM((rows, width), F32)
    scores = local_call(first_body, pltpu.VMEM((rows, planes), F32), (rotated, powers, near, *mine), [stack])
    theirs, scores = lax.optimization_barrier((theirs, scores))
    block = (rings, TOP, folded_width(rotations, width) + 2 * LANES)
    send, soft, by_class, digits = local_call(
        functools.partial(second_body, digit_bits),
        (
            pltpu.VMEM(block, BF16),
            pltpu.VMEM((rows, planes), BF16),
            pltpu.VMEM((2 * (rings + -rings % 8), LANES), BF16),
            pltpu.VMEM((TOP, LANES), F32),
        ),
        (rotated, powers, squares, data_power, prior, scores, far, *theirs),
        [stack],
    )
    arrived = move(send, swap)
    keep = local_call(third_body, pltpu.VMEM(block, F32), (rotated, squares, soft, by_class, digits), [])
    arrived, keep = lax.optimization_barrier((arrived, keep))
    pair = keep + arrived.astype(F32)
    gathered = [pair[0]]
    for d in range(1, rings):
        value = pair[d].astype(BF16)
        value = move(value, shift(rings - d))
        gathered.append(value.astype(F32))
    owned = tree(gathered)
    low = owned.astype(BF16)
    parts = [low]
    for mask in range(1, chips):
        parts.append(move(low, hop(mask)))
    owned = pairwise([part.astype(F32) for part in parts])
    other = move(owned, swap)
    scale = np.zeros((1, LANES), np.float64)
    for j in range(-(-31 // digit_bits)):
        scale[0, j] = 2.0 ** (j * digit_bits - FIXED)
    scale = scale / (count * rings * spread * width)
    sums, ctf_power, log_evidence = finish(owned, other, rotations, width, jnp.asarray(scale, F32))
    return sums.reshape(1, rotations, 2 * width), ctf_power, log_evidence.reshape(())


def solution(mesh):
    return jax.shard_map(
        shards,
        mesh=mesh,
        in_specs=(
            P(("gx", "gy"), None),
            P("gx", None, None),
            P(),
            P(),
            P(),
            P(("gx", "gy")),
            P(),
            P(),
        ),
        out_specs=(P("gx", None, None), P("gx", None), P()),
        check_vma=False,
    )
```

```python
import functools
import math

import jax
import jax.numpy as jnp
import numpy as np
from jax import lax
from jax.experimental import pallas as pl
from jax.experimental.pallas import tpu as pltpu
from jax.sharding import PartitionSpec as P

F32 = jnp.float32
BF16 = jnp.bfloat16
LANES = 128
TOP = 8
FIXED = 6


def own_half():
    place = lax.axis_index("gy")
    half = (place & 1) ^ (lax.axis_index("gx") & 1)
    for bit in range(1, (lax.axis_size("gy") - 1).bit_length()):
        half = half ^ ((place >> bit) & 1)
    return half


def dft_tables(side):
    half = side // 2
    fold = LANES // half
    outer = side // fold
    per_row = LANES // side
    y_hi, parity, x = np.meshgrid(np.arange(fold), np.arange(per_row), np.arange(side), indexing="ij")
    y_hi, parity, x = y_hi.reshape(-1, 1), parity.reshape(-1, 1), x.reshape(-1, 1)
    out_par, part, u_lo, v = np.meshgrid(
        np.arange(per_row), np.arange(2), np.arange(fold), np.arange(half), indexing="ij"
    )
    out_par, part, u_lo, v = (t.reshape(1, -1) for t in (out_par, part, u_lo, v))
    turns = (v * x + outer * u_lo * y_hi) % side
    angle = 2.0 * np.pi * turns / side
    table = np.where(part == 0, np.cos(angle), -np.sin(angle)) / side
    table = np.where(parity == out_par, table, 0.0).astype(np.float32)
    high = table.astype(BF16)
    low = (table - high.astype(np.float32)).astype(BF16)
    pair = np.concatenate([high, low], axis=0)
    lane_u = np.arange(LANES) // half
    turn = (np.arange(outer)[:, None] * lane_u[None, :]) % side
    angle = 2.0 * np.pi * turn / side
    twiddle = np.stack([np.cos(angle), np.sin(angle)], 1).astype(np.float32)
    turn = 2.0 * np.pi * np.arange(side) / side
    wave = np.concatenate([np.cos(turn), np.sin(turn)]).astype(np.float32)
    return pair, twiddle.reshape(2 * outer, LANES), np.tile(wave[None], (8, 1))


def butterflies(real, imag):
    count = len(real)
    if count == 1:
        return real, imag
    even_r, even_i = butterflies(real[0::2], imag[0::2])
    odd_r, odd_i = butterflies(real[1::2], imag[1::2])
    top_r, top_i, low_r, low_i = [], [], [], []
    for k in range(count // 2):
        c = math.cos(2.0 * math.pi * k / count)
        s = math.sin(2.0 * math.pi * k / count)
        r, i = odd_r[k], odd_i[k]
        if k == 0:
            tr, ti = r, i
        elif 4 * k == count:
            tr, ti = i, -r
        elif 8 * k == count:
            tr, ti = (r + i) * c, (i - r) * c
        elif 8 * k == 3 * count:
            tr, ti = (i - r) * s, -(r + i) * s
        else:
            tr, ti = r * c + i * s, i * c - r * s
        top_r.append(even_r[k] + tr)
        top_i.append(even_i[k] + ti)
        low_r.append(even_r[k] - tr)
        low_i.append(even_i[k] - ti)
    return top_r + low_r, top_i + low_i


def split(value):
    high = value.astype(BF16)
    return high, (value - high.astype(F32)).astype(BF16)


def spectra_body(
    ids_near, offsets_near, slots_near, priors_near, images, pair, twiddle, wave, ctf, noise,
    rotated, squares, powers, data_power, prior,
    ids, partial, rows, w_real, w_imag, cosine, sine, inverse, total, arrived,
):
    copy = pltpu.make_async_copy(ids_near, ids, arrived.at[0])
    copy.start()
    count, pixels = images.shape
    side = math.isqrt(pixels)
    half = side // 2
    fold = LANES // half
    outer = side // fold
    per_row = LANES // side
    groups = outer // per_row
    shifts = cosine.shape[0]
    columns = noise.shape[1] // LANES

    tall = []
    for m in range(groups):
        tall.append(jnp.concatenate(
            [images[:, (m + groups * y) * LANES:(m + groups * y + 1) * LANES] for y in range(fold)], axis=1
        ))
    tall = jnp.concatenate(tall, axis=0)
    partial[...] = jnp.dot(jnp.concatenate([tall, tall], axis=1), pair[...], preferred_element_type=F32)
    inverse[...] = 1.0 / noise[...]
    lane = lax.broadcasted_iota(jnp.int32, (shifts, LANES), 1)
    shift = lax.broadcasted_iota(jnp.int32, (shifts, LANES), 0)
    step_u = jnp.zeros((shifts, LANES), jnp.int32)
    step_v = jnp.zeros((shifts, LANES), jnp.int32)
    for s in range(shifts):
        step_u = jnp.where(shift == s, offsets_near[0:1, s:s + 1], step_u)
        step_v = jnp.where(shift == s, offsets_near[1:2, s:s + 1], step_v)
    for column in range(columns):
        u = lane // half + fold * column
        turn = (u * step_u + (lane % half) * step_v) & (side - 1)
        at = slice(column * LANES, (column + 1) * LANES)
        cosine[:, at] = jnp.take_along_axis(wave[...], turn, axis=1)
        sine[:, at] = jnp.take_along_axis(wave[...], turn + side, axis=1)

    classes = slots_near.shape[1]
    scored = prior.shape[0]
    rest = scored // classes - TOP
    line = lax.broadcasted_iota(jnp.int32, prior.shape, 0)
    owner = jnp.where(line < classes * TOP, line // TOP, (line - classes * TOP) // rest)
    slot = lax.rem(lax.axis_index("gx") - owner + classes, classes)
    value = jnp.zeros(prior.shape, F32)
    by_slot = jnp.zeros((1, classes), F32)
    for d in range(classes):
        by_slot = jnp.where(slots_near[...] == d, priors_near[:, d:d + 1], by_slot)
    for d in range(classes):
        value = jnp.where(slot == d, by_slot[:, d:d + 1], value)
    prior[...] = value
    copy.wait()

    def transform(block, carry):
        base = block * 8
        for p in range(8):
            rows[pl.ds(base + p, 1), :] = ctf[pl.ds(ids[base + p], 1), :]
        real, imag = [], []
        for y in range(outer):
            m, parity = y // per_row, y % per_row
            row = pl.ds(m * count + base, 8)
            r = partial[row, (2 * parity) * LANES:(2 * parity + 1) * LANES]
            i = partial[row, (2 * parity + 1) * LANES:(2 * parity + 2) * LANES]
            if y:
                c = twiddle[2 * y:2 * y + 1, :]
                s = twiddle[2 * y + 1:2 * y + 2, :]
                r, i = r * c + i * s, i * c - r * s
            real.append(r)
            imag.append(i)
        real, imag = butterflies(real, imag)
        here = pl.ds(base, 8)
        energy = jnp.zeros((8, LANES), F32)
        for column in range(columns):
            at = slice(column * LANES, (column + 1) * LANES)
            inv = inverse[:, at]
            whiten = rows[here, at] * inv
            r, i = real[column], imag[column]
            energy += (r * r + i * i) * inv
            w_real[here, at] = (r * whiten).astype(BF16).astype(F32)
            w_imag[here, at] = (i * whiten).astype(BF16).astype(F32)
        total[here, :] = energy
        return carry

    lax.fori_loop(0, count // 8, transform, 0, unroll=4)
    energy = jnp.sum(jnp.transpose(total[...]), axis=0, keepdims=True)
    data_power[...] = jnp.concatenate([energy] * (data_power.shape[1] // count), axis=1)

    def rotate(column, carry):
        at = pl.ds(pl.multiple_of(column * LANES, LANES), LANES)
        square = rows[:, at] * rows[:, at]
        high, low = split(square)
        squares[column, 0:count, :] = high
        squares[column, count:, :] = low
        high, low = split(square * inverse[:, at])
        powers[column, 0:count, :] = high
        powers[column, count:, :] = low
        wr, wi = w_real[:, at], w_imag[:, at]
        for s in range(shifts):
            c, n = cosine[s:s + 1, at], sine[s:s + 1, at]
            rotated[column, s * count:(s + 1) * count, :] = (wr * c - wi * n).astype(BF16)
            rotated[columns + column, s * count:(s + 1) * count, :] = (wi * c + wr * n).astype(BF16)
        return carry

    lax.fori_loop(0, columns, rotate, 0, unroll=8)


def spectra(group_ids, particles, shift_offsets, ctf_table, noise_power, slot_class, log_prior, rotations):
    count, pixels = particles.shape
    side = math.isqrt(pixels)
    width = noise_power.shape[0]
    shifts = shift_offsets.shape[0]
    pair, twiddle, wave = dft_tables(side)
    vmem = pl.BlockSpec(memory_space=pltpu.VMEM)
    shape = pltpu.VMEM
    columns = width // LANES
    plane = shape((columns, 2 * count, LANES), BF16)
    scored = shape((slot_class.shape[0] * rotations, LANES), F32)
    k = pair.shape[0] // 2
    groups = pixels // k
    return pl.pallas_call(
        spectra_body,
        out_shape=(shape((2 * columns, shifts * count, LANES), BF16), plane, plane, shape((1, 2 * count), F32), scored),
        cost_estimate=pl.CostEstimate(flops=2**32, transcendentals=0, bytes_accessed=2**23),
        in_specs=[vmem] * 10,
        out_specs=(vmem,) * 5,
        scratch_shapes=[
            pltpu.SMEM(group_ids.shape, jnp.int32),
            pltpu.VMEM((groups * count, pair.shape[1]), F32),
            pltpu.VMEM((count, width), F32),
            pltpu.VMEM((count, width), F32),
            pltpu.VMEM((count, width), F32),
            pltpu.VMEM((shifts, width), F32),
            pltpu.VMEM((shifts, width), F32),
            pltpu.VMEM((1, width), F32),
            pltpu.VMEM((count, LANES), F32),
            pltpu.SemaphoreType.DMA((1,)),
        ],
        compiler_params=pltpu.CompilerParams(vmem_limit_bytes=24 * 2**20),
        name="spectra",
    )(*(
        pltpu.with_memory_space_constraint(x, pltpu.VMEM)
        for x in (
            group_ids, shift_offsets.T, slot_class.reshape(1, -1), log_prior.reshape(1, -1), particles, jnp.asarray(pair), jnp.asarray(twiddle),
            jnp.asarray(wave), ctf_table, noise_power.reshape(1, width),
        )
    ))


def dot_rows(a, b):
    return lax.dot_general(a, b, (((1,), (1,)), ((), ())), preferred_element_type=F32)


def side_by_side(planes, first, count):
    return jnp.concatenate([planes[first + j] for j in range(count)], axis=1)


def fold(value):
    rest = value.shape[0] - TOP
    pieces = TOP // rest
    step = value.shape[1] // pieces
    tail = jnp.concatenate([value[TOP:, j * step:(j + 1) * step] for j in range(pieces)], axis=0)
    return jnp.concatenate([value[:TOP], tail], axis=1)


def folded_width(rotations, width):
    return width + (rotations - TOP) * width // TOP


def fetch_body(far, near, arrived):
    width = near.shape[2]
    h = own_half()
    copies = []
    for j, half in enumerate((h, 1 - h)):
        source = far.at[0, :, pl.ds(pl.multiple_of(half * width, width), width)]
        copies.append(pltpu.make_async_copy(source, near.at[j], arrived.at[j]))
    for copy in copies:
        copy.start()
    for copy in copies:
        copy.wait()


def pack_body(near, mine, theirs):
    for j, out in enumerate((mine, theirs)):
        out[...] = fold(near[j].astype(F32)).astype(BF16)


def pack(references):
    _, rotations, full = references.shape
    width = full // 2
    vmem = pl.BlockSpec(memory_space=pltpu.VMEM)
    near = pl.pallas_call(
        fetch_body,
        out_shape=pltpu.VMEM((2, rotations, width), BF16),
        in_specs=[pl.BlockSpec(memory_space=pltpu.HBM)],
        out_specs=vmem,
        scratch_shapes=[pltpu.SemaphoreType.DMA((2,))],
        compiler_params=pltpu.CompilerParams(vmem_limit_bytes=4 * 2**20),
        name="fetch",
    )(pltpu.with_memory_space_constraint(references, pltpu.HBM))
    out = pltpu.VMEM((TOP, folded_width(rotations, width)), BF16)
    return pl.pallas_call(
        pack_body,
        out_shape=(out, out),
        in_specs=[vmem],
        out_specs=(vmem, vmem),
        cost_estimate=pl.CostEstimate(flops=2**33, transcendentals=0, bytes_accessed=2**20),
        compiler_params=pltpu.CompilerParams(vmem_limit_bytes=4 * 2**20),
        name="pack",
    )(pltpu.with_memory_space_constraint(near, pltpu.VMEM))


def half_scores(h, rotated, powers, packed, stack):
    classes = len(packed)
    rows, width = stack.shape
    rest = rows // classes - TOP
    pieces = TOP // rest
    step = width // pieces
    for d, ref in enumerate(packed):
        value = ref[...].astype(F32)
        stack[d * TOP:(d + 1) * TOP, :] = value[:, :width]
        low = classes * TOP + d * rest
        for j in range(pieces):
            stack[low:low + rest, j * step:(j + 1) * step] = value[j * rest:(j + 1) * rest, width:]
    planes = width // LANES
    value = stack[...]
    inter = dot_rows(value.astype(BF16), side_by_side(rotated, h * planes, planes))
    high, low = split(value * value)
    power = dot_rows(jnp.concatenate([high, low], axis=0), side_by_side(powers, 0, planes))
    power = power[:rows] + power[rows:]
    power = 0.5 * (power + pltpu.roll(power, power.shape[1] // 2, axis=1))
    return [inter[:, j:j + LANES] - power for j in range(0, inter.shape[1], LANES)]


def first_body(rotated, powers, *refs):
    *packed, scores, stack = refs
    parts = half_scores(own_half(), rotated, powers, packed, stack)
    for j, part in enumerate(parts):
        scores[:, j * LANES:(j + 1) * LANES] = part


def half_sums(half, soft, by_class, digits, rotated, squares, out):
    classes = out.shape[0]
    rows = soft.shape[0]
    rest = rows // classes - TOP
    planes = rotated.shape[0] // 2
    width = planes * LANES
    pieces = TOP // rest
    step = width // pieces
    sums = jnp.dot(soft, side_by_side(rotated, half * planes, planes), preferred_element_type=F32)
    narrow = planes // 2
    extra = jnp.dot(by_class, side_by_side(squares, half * narrow, narrow), preferred_element_type=F32)
    extra = extra[:classes] + extra[extra.shape[0] // 2:extra.shape[0] // 2 + classes]
    at = width + step
    for d in range(classes):
        out[d, :, 0:width] = sums[d * TOP:(d + 1) * TOP, :].astype(out.dtype)
        low = sums[classes * TOP + d * rest:classes * TOP + (d + 1) * rest, :]
        tail = jnp.concatenate([low[:, j * step:(j + 1) * step] for j in range(pieces)], axis=0)
        out[d, :, width:at] = tail.astype(out.dtype)
        lines = extra[d:d + 1, :]
        tall = jnp.concatenate([lines[:, j * LANES:(j + 1) * LANES] for j in range(narrow)], axis=0)
        out[d, :, at:at + LANES] = tall.astype(out.dtype)
        out[d, :, at + LANES:at + 2 * LANES] = digits.astype(out.dtype)


def second_body(digit_bits, rotated, powers, squares, data_power, prior, scores, *refs):
    *packed, send, soft_out, class_out, digits_out, stack = refs
    classes = len(packed)
    rows = scores.shape[0]
    rest = rows // classes - TOP
    count = powers.shape[1] // 2
    there = 1 - own_half()
    parts = half_scores(there, rotated, powers, packed, stack)
    energy = 0.5 * data_power[...]
    logits = [
        ((scores[:, j * LANES:(j + 1) * LANES] + part) - energy) + prior[...] for j, part in enumerate(parts)
    ]
    top = jnp.max(functools.reduce(jnp.maximum, logits), axis=0, keepdims=True)
    top = jnp.maximum(top, pltpu.roll(top, count, axis=1))
    raised = [jnp.exp(l - top) for l in logits]
    norm = jnp.sum(functools.reduce(jnp.add, raised), axis=0, keepdims=True)
    norm = norm + pltpu.roll(norm, count, axis=1)
    scale = 1.0 / norm
    weights = [r * scale for r in raised]
    soft = jnp.concatenate([w.astype(BF16) for w in weights], axis=1)
    soft_out[...] = soft

    weight = functools.reduce(jnp.add, weights)
    weight = weight + pltpu.roll(weight, count, axis=1)
    base = classes * TOP
    per_class = jnp.concatenate(
        [
            jnp.sum(weight[d * TOP:(d + 1) * TOP], axis=0, keepdims=True)
            + jnp.sum(weight[base + d * rest:base + (d + 1) * rest], axis=0, keepdims=True)
            for d in range(classes)
        ]
        + [jnp.zeros((-classes % 8, LANES), F32)] * (1 if classes % 8 else 0),
        axis=0,
    )
    high = per_class.astype(BF16).astype(F32)
    lane = lax.broadcasted_iota(jnp.int32, per_class.shape, 1)
    by_class = jnp.concatenate([high, jnp.where(lane < count, per_class - high, 0.0)], axis=0).astype(BF16)
    class_out[...] = by_class

    lane = lax.broadcasted_iota(jnp.int32, (1, LANES), 1)
    evidence = jnp.sum(jnp.where(lane < count, top + jnp.log(norm), 0.0), axis=1, keepdims=True)
    number = jnp.round(jnp.broadcast_to(evidence, (1, LANES)) * float(2**FIXED)).astype(jnp.int32)
    digit = lax.shift_right_logical(jnp.abs(number), jnp.minimum(lane * digit_bits, 31))
    digit = jnp.where(lane * digit_bits < 31, digit & (2**digit_bits - 1), 0)
    digit = jnp.where(number < 0, -digit, digit).astype(F32)
    digits = jnp.broadcast_to(digit, (TOP, LANES))
    digits_out[...] = digits
    half_sums(there, soft, by_class, digits, rotated, squares, send)


def third_body(rotated, squares, soft, by_class, digits, keep):
    half_sums(own_half(), soft[...], by_class[...], digits[...], rotated, squares, keep)


def local_call(body, out_shape, operands, scratch):
    chip = pl.BlockSpec(memory_space=pltpu.VMEM)
    return pl.pallas_call(
        body,
        out_shape=out_shape,
        in_specs=[chip] * len(operands),
        out_specs=jax.tree.map(lambda _: chip, out_shape, is_leaf=lambda x: not isinstance(x, tuple)),
        scratch_shapes=scratch,
        compiler_params=pltpu.CompilerParams(vmem_limit_bytes=16 * 2**20),
        cost_estimate=pl.CostEstimate(flops=2**31, transcendentals=0, bytes_accessed=2**21),
    )(*(pltpu.with_memory_space_constraint(x, pltpu.VMEM) for x in operands))


def finish_body(owned, other, scale, sums, ctf_power, log_evidence):
    rotations, _, full = sums.shape
    width = full // 2
    rest = rotations - TOP
    pieces = TOP // rest
    step = width // pieces
    at = width + step
    narrow = width // 2
    h = own_half()
    for half, source in ((h, owned), (1 - h, other)):
        sums[0:TOP, 0, pl.ds(pl.multiple_of(half * width, width), width)] = source[:, :width]
        for j in range(pieces):
            here = pl.ds(pl.multiple_of(half * width + j * step, step), step)
            sums[TOP:, 0, here] = source[j * rest:(j + 1) * rest, width:at]
        for j in range(narrow // LANES):
            here = pl.ds(pl.multiple_of(half * narrow + j * LANES, LANES), LANES)
            ctf_power[:, here] = source[j:j + 1, at:at + LANES]
    log_evidence[...] = jnp.sum(owned[0:1, at + LANES:at + 2 * LANES] * scale[...], axis=1, keepdims=True)


def finish(owned, other, rotations, width, scale):
    vmem = pl.BlockSpec(memory_space=pltpu.VMEM)
    shape = jax.ShapeDtypeStruct
    return pl.pallas_call(
        finish_body,
        out_shape=(shape((rotations, 1, 2 * width), F32), shape((1, width), F32), shape((1, 1), F32)),
        in_specs=[vmem] * 3,
        out_specs=(vmem,) * 3,
        compiler_params=pltpu.CompilerParams(vmem_limit_bytes=8 * 2**20),
        name="finish",
    )(owned, other, scale)


def tree(parts):
    while len(parts) > 1:
        middle = len(parts) // 2
        parts = [parts[j] + parts[j + middle] for j in range(middle)]
    return parts[0]


def pairwise(parts):
    while len(parts) > 1:
        parts = [a + b for a, b in zip(parts[0::2], parts[1::2], strict=True)]
    return parts[0]


def shards(
    particles, references, slot_class, log_prior, shift_offsets, group_ids, ctf_table, noise_power
):
    rings = lax.axis_size("gx")
    spread = lax.axis_size("gy")
    chips = spread // 2
    count = particles.shape[0]
    width = noise_power.shape[0]
    rotations = references.shape[1]
    digit_bits = max(1, 8 - (rings * spread - 1).bit_length())

    def move(value, rule):
        pairs = []
        for z in range(rings):
            for c in range(chips):
                for core in range(2):
                    z2, c2, core2 = rule(z, c, core)
                    pairs.append((z * spread + 2 * c + core, z2 * spread + 2 * c2 + core2))
        return lax.ppermute(value, ("gx", "gy"), pairs)

    def shift(d):
        return lambda z, c, core: ((z + d) % rings, c, core ^ (d & 1))

    def swap(z, c, core):
        return z, c, core ^ 1

    def hop(mask):
        return lambda z, c, core: (z, c ^ mask, core ^ (bin(mask).count("1") & 1))

    near, far = pack(references)
    mine = []
    for d in range(1, rings):
        mine.append(move(near, shift(d)))
    spectra_out = spectra(
        group_ids, particles, shift_offsets, ctf_table, noise_power, slot_class, log_prior, rotations
    )
    mine, near, far, spectra_out = lax.optimization_barrier((mine, near, far, spectra_out))
    rotated, squares, powers, data_power, prior = spectra_out
    theirs = [move(value, swap) for value in mine]
    rows = rings * rotations
    planes = rotated.shape[1]
    stack = pltpu.VMEM((rows, width), F32)
    scores = local_call(first_body, pltpu.VMEM((rows, planes), F32), (rotated, powers, near, *mine), [stack])
    theirs, scores = lax.optimization_barrier((theirs, scores))
    block = (rings, TOP, folded_width(rotations, width) + 2 * LANES)
    send, soft, by_class, digits = local_call(
        functools.partial(second_body, digit_bits),
        (
            pltpu.VMEM(block, BF16),
            pltpu.VMEM((rows, planes), BF16),
            pltpu.VMEM((2 * (rings + -rings % 8), LANES), BF16),
            pltpu.VMEM((TOP, LANES), F32),
        ),
        (rotated, powers, squares, data_power, prior, scores, far, *theirs),
        [stack],
    )
    arrived = move(send, swap)
    keep = local_call(third_body, pltpu.VMEM(block, F32), (rotated, squares, soft, by_class, digits), [])
    arrived, keep = lax.optimization_barrier((arrived, keep))
    pair = keep + arrived.astype(F32)
    gathered = [pair[0]]
    for d in range(1, rings):
        value = pair[d].astype(BF16)
        value = move(value, shift(rings - d))
        gathered.append(value.astype(F32))
    owned = tree(gathered)
    low = owned.astype(BF16)
    parts = [low]
    for mask in range(1, chips):
        parts.append(move(low, hop(mask)))
    owned = pairwise([part.astype(F32) for part in parts])
    other = move(owned, swap)
    scale = np.zeros((1, LANES), np.float64)
    for j in range(-(-31 // digit_bits)):
        scale[0, j] = 2.0 ** (j * digit_bits - FIXED)
    scale = scale / (count * rings * spread * width)
    sums, ctf_power, log_evidence = finish(owned, other, rotations, width, jnp.asarray(scale, F32))
    return sums.reshape(1, rotations, 2 * width), ctf_power, log_evidence.reshape(())


def solution(mesh):
    return jax.shard_map(
        shards,
        mesh=mesh,
        in_specs=(
            P(("gx", "gy"), None),
            P("gx", None, None),
            P(),
            P(),
            P(),
            P(("gx", "gy")),
            P(),
            P(),
        ),
        out_specs=(P("gx", None, None), P("gx", None), P()),
        check_vma=False,
    )
```
